512 devices in a mesh: dp: 16 (over y, core), ctx: 32 (over z, x).
Axes of the slice: x: 4, y: 8, z: 8, core: 2. Of those that a mesh axis runs over, the one named last changes fastest.
Arguments:
- queries: bfloat16 [16, 4096, 4096], P('dp', 'ctx'), may hold values from -9 to 9
- keys: bfloat16 [16, 4096, 1024], P('dp', 'ctx'), may hold values from -9 to 9
- values: bfloat16 [16, 4096, 1024], P('dp', 'ctx'), may hold values from -6 to 6
- doc_lengths: int32 [16, 128], P('dp'), may hold values from 1 to 128, as said below
- cotangent: float32 [16, 128, 4096], P('dp', 'ctx'), may hold values from -50 to 50
- query_gain: float32 [128], replicated, may hold values from 0.6 to 4.5
- key_gain: float32 [128], replicated, may hold values from 0.6 to 4.5
Outputs:
- embed_quarter: float32 [16, 128, 1024], P('dp', 'ctx')
- embed_half: float32 [16, 128, 2048], P('dp', 'ctx')
- embed_full: float32 [16, 128, 4096], P('dp', 'ctx')
- grad_queries: bfloat16 [16, 4096, 4096], P('dp', 'ctx')
- grad_keys: bfloat16 [16, 4096, 1024], P('dp', 'ctx')
- grad_values: bfloat16 [16, 4096, 1024], P('dp', 'ctx')
- grad_query_gain: float32 [128], replicated
- grad_key_gain: float32 [128], replicated
The draws below stay inside these ranges and needn't reach their ends.
Inputs may be any that keep to these rules, and one draw needn't show every extreme that they name: `doc_lengths`: each sequence's 128 lengths sum to 4096; the first of them is exactly 128. The last 65 documents of each sequence together span at most 128 tokens.
All inputs are finite; a program needn't handle non-finite values.
Results may differ from the reference program's by a relative error of at most 0.0054.
The reference program's roundings to bfloat16 on the way count: a program that leaves them out, or rounds other values in their place, can miss the bound.
Values may be sent and summed in bfloat16 or wider, within the bound.
A program may use at most 64 MiB of HBM per device.

```python
import math
import jax
import jax.numpy as jnp
from jax import lax

QUERY_HEADS = 32
KEY_VALUE_HEADS = 8
HEAD_SIZE = 128
S_DEV = 128
KVW = 1024
MOST = 128
SEQUENCE_TOKENS = 4096
NDOC = 128
PACKED_BATCH = 16
N_CTX = 32


def joint_fields(key):
    base = jax.random.fold_in(key, 101)
    key_q, key_k = jax.random.split(base, 2)
    q_shape = (PACKED_BATCH, SEQUENCE_TOKENS, QUERY_HEADS * HEAD_SIZE)
    key_layout_shape = (PACKED_BATCH, SEQUENCE_TOKENS, KEY_VALUE_HEADS * HEAD_SIZE)
    query_vals = jnp.clip(jax.random.normal(key_q, q_shape, jnp.float32), -6.0, 6.0)
    key_vals = jnp.clip(jax.random.normal(key_k, key_layout_shape, jnp.float32), -6.0, 6.0)
    return (query_vals, key_vals)


def draw_queries(key, part):
    return joint_fields(key)[0].astype(jnp.bfloat16)


def draw_keys(key, part):
    return joint_fields(key)[1].astype(jnp.bfloat16)


def gain_field(key):
    return jax.random.uniform(key, (HEAD_SIZE,), jnp.float32, 0.6, 1.6)


def draw_query_gain(key, part):
    return gain_field(jax.random.fold_in(key, 201))


def draw_key_gain(key, part):
    return gain_field(jax.random.fold_in(key, 202))


def draw_cotangent(key, part):
    inner_key = jax.random.fold_in(key, 301)
    shape = (PACKED_BATCH, NDOC, QUERY_HEADS * HEAD_SIZE)
    ramp = jnp.arange(NDOC, dtype=jnp.float32) / (NDOC - 1)
    lift = jnp.arange(PACKED_BATCH, dtype=jnp.float32) / (PACKED_BATCH - 1)
    scale = jnp.exp(math.log(3.0) * (ramp[None, :, None] + lift[:, None, None]))
    field = jnp.clip(jax.random.normal(inner_key, shape, jnp.float32), -5.0, 5.0)
    return field * scale


def draw_doc_lengths(key, part):
    inner_key = jax.random.fold_in(key, 401)
    key_head, key_delta, key_order = jax.random.split(inner_key, 3)
    leading = NDOC // 2 + 1
    trailing = NDOC - leading
    extra = (S_DEV - leading) // leading
    head = 1 + jax.random.randint(key_head, (PACKED_BATCH, leading), 0, extra + 1)
    remain = SEQUENCE_TOKENS - jnp.sum(head, axis=1, keepdims=True)
    others = trailing - 1
    spread = remain - MOST
    base = spread // others
    left = spread - base * others
    places = jnp.arange(others, dtype=jnp.int32)[None, :]
    fill = base + (places < left).astype(jnp.int32)
    margin = jnp.maximum(jnp.minimum(base - 1, MOST - base - 1), 0)
    pairs = others // 2
    delta = jax.random.randint(key_delta, (PACKED_BATCH, pairs), -margin, margin + 1)
    adjust = jnp.zeros((PACKED_BATCH, others), jnp.int32)
    adjust = adjust.at[:, 0:2 * pairs:2].add(delta).at[:, 1:2 * pairs:2].add(-delta)
    middle = fill + adjust
    order = jax.vmap(lambda single: jax.random.permutation(single, others))(jax.random.split(key_order, PACKED_BATCH))
    middle = jnp.take_along_axis(middle, order, axis=1)
    first = jnp.full((PACKED_BATCH, 1), MOST, jnp.int32)
    return jnp.concatenate([first, middle, head], axis=1).astype(jnp.int32)


def levels(own_key, extent, cuts, low, largest):
    level = 1.0
    for dim, parts in cuts:
        steps = jax.random.uniform(jax.random.fold_in(jax.random.fold_in(own_key, 6), dim), (parts,), jnp.float32, low / len(cuts), largest / len(cuts))
        level = level * jnp.repeat(jnp.exp(steps), extent[dim] // parts).reshape((-1,) + (1,) * (len(extent) - 1 - dim))
    return level


def bell_draw(key, shape, scale, limit, pieces=(), kind=jnp.bfloat16):
    factor_of = levels(key, shape, pieces, -0.22, 0.18) if pieces else 1.0
    drawn = jax.random.normal(key, shape, jnp.float32) * scale * factor_of
    return jnp.minimum(jnp.maximum(drawn, -limit), limit).astype(kind)


def setup_inputs(seed: int = 0) -> dict:
    seeds = jax.random.split(jax.random.key(seed), 8)
    return {
        "queries": draw_queries(jax.random.fold_in(seeds[7], 71), 0),
        "keys": draw_keys(jax.random.fold_in(seeds[7], 71), 0),
        "values": bell_draw(seeds[2], (PACKED_BATCH, SEQUENCE_TOKENS, KVW), 1.0, 6.0, ((0, 16), (1, 32))),
        "doc_lengths": draw_doc_lengths(jax.random.fold_in(seeds[7], 71), 0),
        "cotangent": draw_cotangent(jax.random.fold_in(seeds[7], 71), 0),
        "query_gain": draw_query_gain(jax.random.fold_in(seeds[7], 71), 0),
        "key_gain": draw_key_gain(jax.random.fold_in(seeds[7], 71), 0),
    }


EPS = 1e-06

def widen(field):
    return lax.optimization_barrier(field).astype(jnp.float32)

def rms_forward(field, gain):
    inverse = lax.rsqrt(lax.optimization_barrier(jnp.mean(field * field, axis=-1, keepdims=True)) + EPS)
    unit = field * inverse
    return (unit * gain, unit, inverse)

def rms_backward(grad, unit, inverse, gain):
    scaled = grad * gain
    inner = lax.optimization_barrier(jnp.mean(scaled * unit, axis=-1, keepdims=True))
    grad_in = inverse * (scaled - unit * inner)
    grad_gain = lax.optimization_barrier(jnp.sum((grad * unit).reshape(-1, unit.shape[-1]), axis=0))
    return (grad_in, grad_gain)

def doc_ids(lengths, positions, total):
    ends = jnp.cumsum(lengths, dtype=jnp.int32)
    owner = lax.optimization_barrier(jnp.sum((positions[:, None] >= ends[None, :]).astype(jnp.int32), axis=1))
    inside = (positions >= 0) & (positions < total)
    return jnp.where(inside, owner, -1).astype(jnp.int32)

def block_probs(queries, keys, query_ids, key_ids):
    rows, heads, width = queries.shape
    query_groups = keys.shape[1]
    grouped = queries.reshape(rows, query_groups, heads // query_groups, width)
    scores = jnp.einsum('rgpe,kge->gprk', widen(grouped), widen(keys)) * (1.0 / math.sqrt(width))
    allowed = query_ids[:, None] == key_ids[None, :]
    scores = jnp.where(allowed[None, None], scores, -jnp.inf)
    top = lax.optimization_barrier(jnp.max(scores, axis=-1, keepdims=True))
    powers = jnp.exp(scores - top)
    return (powers / lax.optimization_barrier(jnp.sum(powers, axis=-1, keepdims=True)), grouped)

def forward_block(queries, keys, values, query_ids, key_ids):
    probs, grouped = block_probs(queries, keys, query_ids, key_ids)
    low = probs.astype(jnp.bfloat16)
    mixed = jnp.einsum('gprk,kge->rgpe', widen(low), widen(values))
    return mixed.reshape(queries.shape[0], -1).astype(jnp.bfloat16)

def backward_block(queries, keys, values, query_ids, key_ids, grad_out):
    probs, grouped = block_probs(queries, keys, query_ids, key_ids)
    low = probs.astype(jnp.bfloat16)
    rows, heads, width = queries.shape
    query_groups = keys.shape[1]
    grad_four = grad_out.reshape(rows, query_groups, heads // query_groups, width)
    grad_probs = jnp.einsum('rgpe,kge->gprk', widen(grad_four), widen(values))
    inner = lax.optimization_barrier(jnp.sum(probs * grad_probs, axis=-1, keepdims=True))
    grad_scores = (probs * (grad_probs - inner)).astype(jnp.bfloat16)
    scale = 1.0 / math.sqrt(width)
    grad_q = jnp.einsum('gprk,kge->rgpe', widen(grad_scores), widen(keys)) * scale
    grad_k = jnp.einsum('gprk,rgpe->kge', widen(grad_scores), widen(grouped)) * scale
    grad_v = jnp.einsum('gprk,rgpe->kge', widen(low), widen(grad_four))
    return (grad_q.reshape(rows, heads, width), grad_k, grad_v)

def matryoshka(pooled, cotangent):
    width = pooled.shape[-1]
    prefixes = (width // 4, width // 2, width)

    def embed(field):
        return tuple((field[:, :count] * lax.rsqrt(lax.optimization_barrier(jnp.sum(field[:, :count] * field[:, :count], axis=-1, keepdims=True)) + EPS) for count in prefixes))
    embeds, pullback = jax.vjp(embed, pooled)
    grad, = pullback(tuple((cotangent[:, :count] for count in prefixes)))
    return (embeds, grad)

def one_sequence(queries, keys, values, lengths, cotangent, query_gain, key_gain):
    total = S_DEV * N_CTX
    block = min(512, 4 * S_DEV)
    window = block + 2 * S_DEV
    heads = QUERY_HEADS
    query_groups = KEY_VALUE_HEADS
    width = HEAD_SIZE
    normed_f, unit_q, inv_q = rms_forward(queries.astype(jnp.float32).reshape(total, heads, width), query_gain)
    normed_q = normed_f.astype(jnp.bfloat16)
    normed_kf, unit_k, inv_k = rms_forward(keys.astype(jnp.float32).reshape(total, query_groups, width), key_gain)
    normed_k = normed_kf.astype(jnp.bfloat16)
    value_rows = values.reshape(total, query_groups, width)
    token_ids = doc_ids(lengths, jnp.arange(total, dtype=jnp.int32), total)
    pad_ids = doc_ids(lengths, jnp.arange(total + 2 * S_DEV, dtype=jnp.int32) - S_DEV, total)
    key_pad = jnp.pad(normed_k, ((S_DEV, S_DEV), (0, 0), (0, 0)))
    value_pad = jnp.pad(value_rows, ((S_DEV, S_DEV), (0, 0), (0, 0)))
    count = total // block

    def forward(index):
        start = index * block
        return forward_block(lax.dynamic_slice_in_dim(normed_q, start, block, 0), lax.dynamic_slice_in_dim(key_pad, start, window, 0), lax.dynamic_slice_in_dim(value_pad, start, window, 0), lax.dynamic_slice_in_dim(token_ids, start, block, 0), lax.dynamic_slice_in_dim(pad_ids, start, window, 0))
    attended = lax.map(forward, jnp.arange(count, dtype=jnp.int32)).reshape(total, heads * width)
    onehot = (token_ids[:, None] == jnp.arange(NDOC, dtype=jnp.int32)[None, :]).astype(jnp.bfloat16)
    sums = jnp.dot(onehot.T, attended, preferred_element_type=jnp.float32)
    counts = lengths.astype(jnp.float32)[:, None]
    pooled = sums / counts
    embeds, grad_pooled = matryoshka(pooled, cotangent)
    grad_out = jnp.take(grad_pooled / counts, token_ids, axis=0).astype(jnp.bfloat16)
    zeros = jnp.zeros((total + 2 * S_DEV, query_groups, width), jnp.float32)

    def backward(carry, index):
        key_acc, value_acc = carry
        start = index * block
        grad_q, grad_k, grad_v = backward_block(lax.dynamic_slice_in_dim(normed_q, start, block, 0), lax.dynamic_slice_in_dim(key_pad, start, window, 0), lax.dynamic_slice_in_dim(value_pad, start, window, 0), lax.dynamic_slice_in_dim(token_ids, start, block, 0), lax.dynamic_slice_in_dim(pad_ids, start, window, 0), lax.dynamic_slice_in_dim(grad_out, start, block, 0))
        key_acc = lax.dynamic_update_slice_in_dim(key_acc, lax.dynamic_slice_in_dim(key_acc, start, window, 0) + grad_k, start, 0)
        value_acc = lax.dynamic_update_slice_in_dim(value_acc, lax.dynamic_slice_in_dim(value_acc, start, window, 0) + grad_v, start, 0)
        return ((key_acc, value_acc), grad_q)
    (key_acc, value_acc), grad_blocks = lax.scan(backward, (zeros, zeros), jnp.arange(count, dtype=jnp.int32))
    grad_nq = grad_blocks.reshape(total, heads, width)
    grad_nk = key_acc[S_DEV:S_DEV + total]
    grad_values = value_acc[S_DEV:S_DEV + total]
    grad_q, grad_qgain = rms_backward(grad_nq, unit_q, inv_q, query_gain)
    grad_k, grad_kgain = rms_backward(grad_nk, unit_k, inv_k, key_gain)
    return (embeds[0], embeds[1], embeds[2], grad_q.astype(jnp.bfloat16).reshape(total, heads * width), grad_k.astype(jnp.bfloat16).reshape(total, query_groups * width), grad_values.astype(jnp.bfloat16).reshape(total, query_groups * width), grad_qgain, grad_kgain)

def reference(queries, keys, values, doc_lengths, cotangent, query_gain, key_gain):

    def single(packed):
        return one_sequence(packed[0], packed[1], packed[2], packed[3], packed[4], query_gain, key_gain)
    results = lax.map(single, (queries, keys, values, doc_lengths, cotangent))
    return (results[0], results[1], results[2], results[3], results[4], results[5], lax.optimization_barrier(jnp.sum(results[6], axis=0)), lax.optimization_barrier(jnp.sum(results[7], axis=0)))
```

```python
import functools
import math

import jax
import jax.numpy as jnp
from jax import lax
from jax.experimental import pallas as pl
from jax.experimental.pallas import tpu as pltpu
from jax.sharding import PartitionSpec as P

EPS = 1e-06
T = 128
G = 8
R = 4
W = 4096
NX, NZ = 4, 8
C = 1024
SCALE = 1.0 / math.sqrt(T)
LOG2E = 1.4426950408889634
NEG = -1e30
F32, BF16 = jnp.float32, jnp.bfloat16
MESH = pl.DeviceIdType.MESH
LAST = NX * NZ - 1
HALF = NX * NZ // 2
NT = (((1,), (1,)), ((), ()))
TN = (((0,), (0,)), ((), ()))


def iota(shape, dim):
    return lax.broadcasted_iota(jnp.int32, shape, dim)


def dot(a, b, dims=(((1,), (0,)), ((), ()))):
    return lax.dot_general(a, b, dims, preferred_element_type=F32)


def rows_of(start, size):
    return pl.ds(pl.multiple_of(start, 16), size)


def cols_of(start, size):
    return pl.ds(pl.multiple_of(start, 128), size)


def kernel(
    ny, nc,
    q_ref, k_ref, v_ref, len_ref, cot_ref, qg_ref, kg_ref,
    eq_ref, eh_ref, ef_ref, gq_ref, gk_ref, gv_ref, qgain_ref, kgain_ref,
    halo, kn, uk, ik, vw, qn, uq, iq, pr, bias, att, pool, tokc, ga, rows_s, rows_r,
    blk32, blk, cot_a, cot_b, s2, s2b, rx, zs, rz, rb, dss, lows, dos, dh_s, dh_r, dk_own, dv_own,
    gz, gy, gx,
    h_snd, h_rcv, r_snd, r_rcv, cz_snd, cz_rcv, cx_snd, cx_rcv, cb_snd, cb_rcv,
    px_snd, px_rcv, pz_snd, pz_rcv, pb_snd, pb_rcv, d_snd, d_rcv,
    gz_snd, gz_rcv, gy_snd, gy_rcv, gx_snd, gx_rcv,
):
    dp, ctx = lax.axis_index("dp"), lax.axis_index("ctx")
    z, x = ctx // NX, ctx % NX
    y, core = dp // nc, dp % nc
    nxt, prv = (ctx + 1) % (NX * NZ), (ctx + NX * NZ - 1) % (NX * NZ)
    low_half = z < NZ // 2
    sends_b = jnp.logical_and(ctx >= HALF, ctx < LAST)

    def at_z(i):
        return (dp, ((z + i) % NZ) * NX + x)

    def at_x(i):
        return (dp, z * NX + (x + i) % NX)

    def at_y(i):
        return (((y + i) % ny) * nc + core, ctx)

    barrier = pltpu.get_barrier_semaphore()

    def greet(device):
        pl.semaphore_signal(barrier, inc=1, device_id=device, device_id_type=MESH)

    for i in range(1, NZ):
        greet(at_z(i))
    for i in range(1, NX):
        greet(at_x(i))
    for i in range(1, ny):
        greet(at_y(i))
    for j in range(1, nc):
        for i in range(NX):
            greet((y * nc + (core + j) % nc, z * NX + (x + i) % NX))

    @pl.when(x == NX - 1)
    def _():
        greet((dp, nxt))

    @pl.when(x == 0)
    def _():
        greet((dp, prv))

    @pl.when(sends_b)
    def _():
        greet((dp, LAST))

    @pl.when(ctx == LAST)
    def _():
        @pl.loop(HALF, LAST)
        def _(c):
            greet((dp, c))

    count = (NZ - 1) + (NX - 1) + (ny - 1) + NX * (nc - 1)
    edge = jnp.where(jnp.logical_or(x == 0, x == NX - 1), 1, 0)
    far = jnp.where(ctx == LAST, LAST - HALF, jnp.where(sends_b, 1, 0))
    pl.semaphore_wait(barrier, count + edge + far)

    def remote(src, dst, snd, rcv, device):
        return pltpu.make_async_remote_copy(
            src_ref=src, dst_ref=dst, send_sem=snd, recv_sem=rcv, device_id=device, device_id_type=MESH
        )

    def halo_copy(g, i):
        src = (k_ref if i < 2 else v_ref).at[:, cols_of(g * T, T)]
        return remote(src, halo.at[g, i], h_snd.at[g, i], h_rcv.at[g, i], (dp, nxt if i % 2 == 0 else prv))

    @pl.loop(0, G)
    def _(g):
        for i in range(4):
            halo_copy(g, i).start()

    for c in range(4):
        blk32[c * 4 : c * 4 + 4, :] = cot_ref[:, c * C : (c + 1) * C]
    blk[...] = blk32[...].astype(BF16)

    def cz_copy(i):
        return remote(
            blk, cot_a.at[rows_of(x * 64 + z * 16, 16)], cz_snd.at[i], cz_rcv.at[z], at_z(i)
        )

    def cz_wait(zz):
        return remote(blk, cot_a.at[rows_of(x * 64 + zz * 16, 16)], cz_snd.at[0], cz_rcv.at[zz], at_z(1))

    def cx_copy(i):
        own = cot_a.at[rows_of(x * 64, 64)]
        return remote(own, own, cx_snd.at[i], cx_rcv.at[x], at_x(i))

    def cx_wait(i):
        own = cot_a.at[rows_of(((x + i) % NX) * 64, 64)]
        return remote(own, own, cx_snd.at[i], cx_rcv.at[(x + i) % NX], at_x(i))

    def cb_copy(c):
        return remote(
            blk, cot_b.at[rows_of((c - HALF) * 16, 16)], cb_snd.at[0], cb_rcv.at[c - HALF], (dp, LAST)
        )

    @pl.when(low_half)
    def _():
        cot_a[rows_of(x * 64 + z * 16, 16), :] = blk[...]
        for i in range(1, NZ):
            cz_copy(i).start()

    @pl.when(sends_b)
    def _():
        cb_copy(ctx).start()

    @pl.when(ctx == LAST)
    def _():
        cot_b[(HALF - 1) * 16 : HALF * 16, :] = blk[...]

    lens = jnp.broadcast_to(len_ref[...].astype(F32), (T, T))
    ii, jj = iota((T, T), 0), iota((T, T), 1)
    base = (ctx * T).astype(F32)

    def pick(cond, value, axis):
        return jnp.sum(jnp.where(cond, value, 0.0), axis=axis, keepdims=True)

    lens_col = pick(ii == jj, lens, 1)
    ends_col = pick(jj <= ii, lens, 1)
    ends_row = pick(ii <= jj, jnp.broadcast_to(lens_col, (T, T)), 0)
    starts = ends_row - lens[:1]
    ids_col = pick(base + ii.astype(F32) >= ends_row, 1.0, 1)
    key_pos = base - T + iota((T, 3 * T), 1).astype(F32)
    ids_row = jnp.where(key_pos[:1] < 0.0, -1.0, pick(key_pos >= ends_col, 1.0, 0))
    bias[...] = jnp.where(ids_col == ids_row, 0.0, NEG)
    own_row = ids_row[:, T : 2 * T]
    same = jnp.where(ids_col == own_row, 1.0, 0.0).astype(BF16)
    inv_len = 1.0 / pick(ids_col == jj.astype(F32), lens, 1)
    first_id = jnp.min(own_row, axis=1, keepdims=True)
    last_id = jnp.max(own_row, axis=1, keepdims=True)
    with_prv = jnp.where(ids_col == jnp.max(ids_row[:, :T], axis=1, keepdims=True), 1.0, 0.0)
    with_nxt = jnp.where(ids_col == jnp.min(ids_row[:, 2 * T :], axis=1, keepdims=True), 1.0, 0.0)
    r8 = iota((8, T), 0)
    ends8 = jnp.where(
        jnp.logical_or(
            jnp.logical_and(r8 == 0, own_row == first_id), jnp.logical_and(r8 == 1, own_row == last_id)
        ),
        1.0,
        0.0,
    ).astype(BF16)

    q_gain, k_gain = qg_ref[...], kg_ref[...]

    def forward(g):
        for i in range(4):
            halo_copy(g, i).wait_recv()
        cols = cols_of(g * T, T)
        for i, raw in enumerate((halo[g, 0], k_ref[:, cols], halo[g, 1])):
            raw = raw.astype(F32)
            inv = lax.rsqrt(jnp.mean(raw * raw, axis=-1, keepdims=True) + EPS)
            unit = raw * inv
            uk[g, i * T : (i + 1) * T, :] = unit
            kn[g, i * T : (i + 1) * T, :] = (unit * k_gain).astype(BF16)
            if i == 1:
                ik[g] = inv
        vw[g, :T, :] = halo[g, 2]
        vw[g, T : 2 * T, :] = v_ref[:, cols]
        vw[g, 2 * T :, :] = halo[g, 3]
        for p in range(R):
            cols = cols_of(g * (R * T) + p * T, T)
            rows = slice(p * T, (p + 1) * T)
            raw = q_ref[:, cols].astype(F32)
            inv = lax.rsqrt(jnp.mean(raw * raw, axis=-1, keepdims=True) + EPS)
            unit = raw * inv
            normed = (unit * q_gain).astype(BF16)
            uq[g, rows, :] = unit
            iq[g, rows, :] = inv
            qn[g, rows, :] = normed
            s = dot(normed, kn[g], NT) * (SCALE * LOG2E) + bias[...]
            powers = jnp.exp2(s - jnp.max(s, axis=-1, keepdims=True))
            probs = powers * (1.0 / jnp.sum(powers, axis=-1, keepdims=True))
            pr[g, rows, :] = probs
            att[:, cols] = dot(probs.astype(BF16), vw[g]).astype(BF16)

    @pl.loop(0, G // 2)
    def _(g):
        forward(g)

    for zz in range(NZ // 2):
        @pl.when(z != zz)
        def _():
            cz_wait(zz).wait_recv()
    for i in range(1, NX):
        cx_copy(i).start()

    @pl.loop(G // 2, G)
    def _(g):
        forward(g)

    for c in range(8):
        cols = slice(c * 512, (c + 1) * 512)
        ends = dot(ends8, att[:, cols])
        rows_s[0, :, cols] = ends[0:1]
        rows_s[1, :, cols] = ends[1:2]

    def row_copy(i):
        return remote(rows_s.at[i], rows_r.at[1 - i], r_snd.at[i], r_rcv.at[1 - i], (dp, prv if i == 0 else nxt))

    row_copy(0).start()
    row_copy(1).start()
    for c in range(8):
        cols = slice(c * 512, (c + 1) * 512)
        pool[:, cols] = dot(same, att[:, cols])

    for i in range(1, NX):
        cx_wait(i).wait_recv()
    rr = iota((1, 256), 1)
    doc_a = (((rr >> 4) & 3) * 16 + (rr >> 6) * 4 + (rr & 3)).astype(F32)
    doc_b = (64 + (rr >> 4) * 4 + (rr & 3)).astype(F32)
    quarter = (rr >> 2) & 3
    for c in range(8):
        cols = slice((c % 2) * 512, (c % 2 + 1) * 512)
        hot = jnp.where(jnp.logical_and(ids_col == doc_a, quarter == c // 2), 1.0, 0.0).astype(BF16)
        tokc[:, c * 512 : (c + 1) * 512] = dot(hot, cot_a[:, cols])

    @pl.when(ctx == LAST)
    def _():
        @pl.loop(HALF, LAST)
        def _(c):
            cb_copy(c).wait_recv()
        for c in range(8):
            cols = slice((c % 2) * 512, (c % 2 + 1) * 512)
            hot = jnp.where(jnp.logical_and(ids_col == doc_b, quarter == c // 2), 1.0, 0.0).astype(BF16)
            tokc[:, c * 512 : (c + 1) * 512] += dot(hot, cot_b[:, cols])

    row_copy(0).wait_recv()
    row_copy(1).wait_recv()
    norms, inners = [], []
    for c in range(8):
        cols = slice(c * 512, (c + 1) * 512)
        p = (pool[:, cols] + with_prv * rows_r[0, :, cols] + with_nxt * rows_r[1, :, cols]) * inv_len
        pool[:, cols] = p
        norms.append(jnp.sum(p * p, axis=1, keepdims=True))
        inners.append(jnp.sum(p * tokc[:, cols], axis=1, keepdims=True))

    rc = iota((256, T), 0)
    tc = iota((256, T), 1)
    doc_of = ((rc >> 4) & 3) * 16 + (rc >> 6) * 4 + (rc & 3)
    at_a = pick(doc_of == tc, starts, 1) - base == tc.astype(F32)
    part = (rc >> 2) & 3
    for h in range(2):
        total = None
        for c in range(4):
            hot = jnp.where(jnp.logical_and(at_a, part == c), 1.0, 0.0).astype(BF16)
            term = dot(hot, pool[:, c * C + h * 512 : c * C + (h + 1) * 512].astype(BF16))
            total = term if total is None else total + term
        s2[:, h * 512 : (h + 1) * 512] = total.astype(BF16)

    def px_copy(i):
        return remote(
            s2.at[rows_of(((x + i) % NX) * 64, 64)], rx.at[x], px_snd.at[i], px_rcv.at[x], at_x(i)
        )

    def px_wait(i):
        return remote(s2.at[rows_of(x * 64, 64)], rx.at[(x + i) % NX], px_snd.at[i], px_rcv.at[(x + i) % NX], at_x(i))

    for i in range(1, NX):
        px_copy(i).start()

    def pb_copy(c):
        return remote(s2b.at[rows_of((c - HALF) * 16, 16)], rb, pb_snd.at[c - HALF], pb_rcv.at[0], (dp, c))

    @pl.when(ctx == LAST)
    def _():
        doc_of = 64 + (rc >> 4) * 4 + (rc & 3)
        at_b = pick(doc_of == tc, starts, 1) - base == tc.astype(F32)
        for h in range(2):
            total = None
            for c in range(4):
                hot = jnp.where(jnp.logical_and(at_b, part == c), 1.0, 0.0).astype(BF16)
                term = dot(hot, pool[:, c * C + h * 512 : c * C + (h + 1) * 512].astype(BF16))
                total = term if total is None else total + term
            s2b[:, h * 512 : (h + 1) * 512] = total.astype(BF16)

        @pl.loop(HALF, LAST)
        def _(c):
            pb_copy(c).start()

    by_quarter = [norms[2 * c] + norms[2 * c + 1] for c in range(4)]
    inner_quarter = [inners[2 * c] + inners[2 * c + 1] for c in range(4)]
    n1 = by_quarter[0]
    n2 = n1 + by_quarter[1]
    n4 = n2 + by_quarter[2] + by_quarter[3]
    d1 = inner_quarter[0]
    d2 = d1 + inner_quarter[1]
    d4 = d2 + inner_quarter[2] + inner_quarter[3]
    i1, i2, i4 = lax.rsqrt(n1 + EPS), lax.rsqrt(n2 + EPS), lax.rsqrt(n4 + EPS)
    b1, b2, b4 = i1 * i1 * i1 * d1, i2 * i2 * i2 * d2, i4 * i4 * i4 * d4
    left = [i1 + i2 + i4, i2 + i4, i4, i4]
    right = [b1 + b2 + b4, b2 + b4, b4, b4]
    for c in range(8):
        cols = slice(c * 512, (c + 1) * 512)
        ga[:, cols] = ((left[c // 2] * tokc[:, cols] - right[c // 2] * pool[:, cols]) * inv_len).astype(BF16)

    def grad_copy(g, i):
        return remote(
            dh_s.at[g, i], dh_r.at[g, i], d_snd.at[g, i], d_rcv.at[g, i], (dp, prv if i % 2 == 0 else nxt)
        )

    def backward(g, carry):
        q_sum, k_sum = carry
        for p in range(R):
            cols = cols_of(g * (R * T) + p * T, T)
            rows = slice(p * T, (p + 1) * T)
            do = ga[:, cols]
            dos[rows, :] = do
            probs = pr[g, rows, :]
            dprobs = dot(do, vw[g], NT)
            inner = jnp.sum(probs * dprobs, axis=-1, keepdims=True)
            ds = (probs * (dprobs - inner)).astype(BF16)
            dss[rows, :] = ds
            lows[rows, :] = probs.astype(BF16)
            dq = dot(ds, kn[g]) * SCALE
            unit = uq[g, rows, :]
            q_sum = q_sum + jnp.sum(dq * unit, axis=0, keepdims=True)
            scaled = dq * q_gain
            mean = jnp.mean(scaled * unit, axis=-1, keepdims=True)
            gq_ref[:, cols] = (iq[g, rows, :] * (scaled - unit * mean)).astype(BF16)
        dk = dot(dss[...], qn[g], TN) * SCALE
        dv = dot(lows[...], dos[...], TN)
        k_sum = k_sum + jnp.sum(dk * uk[g], axis=0, keepdims=True)
        dh_s[g, 0] = dk[:T].astype(BF16)
        dh_s[g, 1] = dk[2 * T :].astype(BF16)
        dh_s[g, 2] = dv[:T].astype(BF16)
        dh_s[g, 3] = dv[2 * T :].astype(BF16)
        for i in range(4):
            grad_copy(g, i).start()
        dk_own[g] = dk[T : 2 * T]
        dv_own[g] = dv[T : 2 * T]
        return q_sum, k_sum

    zero = jnp.zeros((1, T), F32)
    sums = lax.fori_loop(0, G // 2, backward, (zero, zero))

    def pz_copy(i):
        return remote(
            zs.at[rows_of(((z + i) % NZ) * 16, 16)], rz.at[z], pz_snd.at[i], pz_rcv.at[z], at_z(i)
        )

    def pz_wait(i):
        return remote(zs.at[rows_of(0, 16)], rz.at[(z + i) % NZ], pz_snd.at[i], pz_rcv.at[(z + i) % NZ], at_z(i))

    def to_low(i):
        return (z + i) % NZ < NZ // 2

    for i in range(1, NX):
        px_wait(i).wait_recv()
    merged = s2[rows_of(x * 64, 64), :].astype(F32)
    for i in range(1, NX):
        merged = merged + rx[(x + i) % NX].astype(F32)
    zs[...] = merged.astype(BF16)
    for i in range(1, NZ):
        @pl.when(to_low(i))
        def _():
            pz_copy(i).start()

    q_sum, k_sum = lax.fori_loop(G // 2, G, backward, sums)

    def total_of(slots, place, count, copies):
        for copy in copies:
            copy[0].start()
        for copy in copies:
            copy[1].wait_recv()
        total = slots[0]
        for i in range(1, count):
            total = total + slots[i]
        return total

    def gain_pair(slots, snd, rcv, i, place, other, device):
        return (
            remote(slots.at[place], slots.at[place], snd.at[i], rcv.at[place], device),
            remote(slots.at[other], slots.at[other], snd.at[i], rcv.at[other], device),
        )

    r8 = iota((8, T), 0)
    gz[z] = jnp.where(r8 == 0, q_sum, jnp.where(r8 == 1, k_sum, 0.0))
    z_pairs = [gain_pair(gz, gz_snd, gz_rcv, i, z, (z + i) % NZ, at_z(i)) for i in range(1, NZ)]
    gy[y] = total_of(gz, z, NZ, z_pairs)
    y_pairs = [gain_pair(gy, gy_snd, gy_rcv, i, y, (y + i) % ny, at_y(i)) for i in range(1, ny)]
    spot = core * NX + x
    gx[spot] = total_of(gy, y, ny, y_pairs)
    x_pairs = []
    for j in range(nc):
        for i in range(NX):
            if i or j:
                there = (core + j) % nc
                other = there * NX + (x + i) % NX
                device = (y * nc + there, z * NX + (x + i) % NX)
                x_pairs.append(gain_pair(gx, gx_snd, gx_rcv, j * NX + i, spot, other, device))
    total = total_of(gx, spot, NX * nc, x_pairs)
    qgain_ref[...] = total[0:1]
    kgain_ref[...] = total[1:2]

    @pl.loop(0, G)
    def _(g):
        for i in range(4):
            grad_copy(g, i).wait_recv()
        cols = cols_of(g * T, T)
        dk = dk_own[g] + (dh_r[g, 0].astype(F32) + dh_r[g, 1].astype(F32))
        dv = dv_own[g] + (dh_r[g, 2].astype(F32) + dh_r[g, 3].astype(F32))
        unit = uk[g, T : 2 * T, :]
        scaled = dk * k_gain
        mean = jnp.mean(scaled * unit, axis=-1, keepdims=True)
        gk_ref[:, cols] = (ik[g] * (scaled - unit * mean)).astype(BF16)
        gv_ref[:, cols] = dv.astype(BF16)

    def embed(rows):
        parts = [rows[c * 4 : c * 4 + 4] for c in range(4)]
        squares = [jnp.sum(part * part, axis=1, keepdims=True) for part in parts]
        m1 = squares[0]
        m2 = m1 + squares[1]
        m4 = m2 + squares[2] + squares[3]
        eq_ref[...] = parts[0] * lax.rsqrt(m1 + EPS)
        for ref, m, count in ((eh_ref, m2, 2), (ef_ref, m4, 4)):
            inv = lax.rsqrt(m + EPS)
            for c in range(count):
                ref[:, c * C : (c + 1) * C] = parts[c] * inv

    @pl.when(low_half)
    def _():
        rows = zs[rows_of(z * 16, 16), :].astype(F32)
        for i in range(1, NZ):
            pz_wait(i).wait_recv()
            rows = rows + rz[(z + i) % NZ].astype(F32)
        embed(rows)

    @pl.when(sends_b)
    def _():
        pb_copy(ctx).wait_recv()
        embed(rb[...].astype(F32))

    @pl.when(ctx == LAST)
    def _():
        embed(s2b[(HALF - 1) * 16 : HALF * 16, :].astype(F32))

    @pl.loop(0, G)
    def _(g):
        for i in range(4):
            halo_copy(g, i).wait_send()
            grad_copy(g, i).wait_send()
    row_copy(0).wait_send()
    row_copy(1).wait_send()
    for i in range(1, NX):
        cx_copy(i).wait_send()
        px_copy(i).wait_send()
    for i in range(1, NZ):
        @pl.when(low_half)
        def _():
            cz_copy(i).wait_send()

        @pl.when(to_low(i))
        def _():
            pz_copy(i).wait_send()

    @pl.when(sends_b)
    def _():
        cb_copy(ctx).wait_send()

    @pl.when(ctx == LAST)
    def _():
        @pl.loop(HALF, LAST)
        def _(c):
            pb_copy(c).wait_send()
    for pair in z_pairs + y_pairs + x_pairs:
        pair[0].wait_send()


def body(queries, keys, values, doc_lengths, cotangent, query_gain, key_gain):
    nc = 2 if lax.axis_size("dp") > 1 else 1
    ny = lax.axis_size("dp") // nc
    vmem, dma = pltpu.VMEM, pltpu.SemaphoreType.DMA
    scratch = [
        vmem((G, 4, T, T), BF16),
        vmem((G, 3 * T, T), BF16),
        vmem((G, 3 * T, T), F32),
        vmem((G, T, 1), F32),
        vmem((G, 3 * T, T), BF16),
        vmem((G, R * T, T), BF16),
        vmem((G, R * T, T), F32),
        vmem((G, R * T, 1), F32),
        vmem((G, R * T, 3 * T), F32),
        vmem((T, 3 * T), F32),
        vmem((T, W), BF16),
        vmem((T, W), F32),
        vmem((T, W), F32),
        vmem((T, W), BF16),
        vmem((2, 1, W), F32),
        vmem((2, 1, W), F32),
        vmem((16, C), F32),
        vmem((16, C), BF16),
        vmem((256, C), BF16),
        vmem((256, C), BF16),
        vmem((256, C), BF16),
        vmem((256, C), BF16),
        vmem((NX, 64, C), BF16),
        vmem((64, C), BF16),
        vmem((NZ, 16, C), BF16),
        vmem((16, C), BF16),
        vmem((R * T, 3 * T), BF16),
        vmem((R * T, 3 * T), BF16),
        vmem((R * T, T), BF16),
        vmem((G, 4, T, T), BF16),
        vmem((G, 4, T, T), BF16),
        vmem((G, T, T), F32),
        vmem((G, T, T), F32),
        vmem((NZ, 8, T), F32),
        vmem((ny, 8, T), F32),
        vmem((nc * NX, 8, T), F32),
        dma((G, 4)), dma((G, 4)),
        dma((2,)), dma((2,)),
        dma((NZ,)), dma((NZ,)),
        dma((NX,)), dma((NX,)),
        dma((1,)), dma((HALF,)),
        dma((NX,)), dma((NX,)),
        dma((NZ,)), dma((NZ,)),
        dma((HALF,)), dma((1,)),
        dma((G, 4)), dma((G, 4)),
        dma((NZ,)), dma((NZ,)),
        dma((ny,)), dma((ny,)),
        dma((nc * NX,)), dma((nc * NX,)),
    ]
    shape = jax.ShapeDtypeStruct
    outs = pl.pallas_call(
        functools.partial(kernel, ny, nc),
        out_shape=(
            shape((4, C), F32),
            shape((4, 2 * C), F32),
            shape((4, W), F32),
            shape((T, W), BF16),
            shape((T, G * T), BF16),
            shape((T, G * T), BF16),
            shape((1, T), F32),
            shape((1, T), F32),
        ),
        in_specs=[pl.BlockSpec(memory_space=pltpu.VMEM)] * 7,
        out_specs=tuple([pl.BlockSpec(memory_space=pltpu.VMEM)] * 8),
        scratch_shapes=scratch,
        compiler_params=pltpu.CompilerParams(
            collective_id=0, has_side_effects=True, vmem_limit_bytes=56 * 1024 * 1024
        ),
    )(
        queries[0], keys[0], values[0], doc_lengths, cotangent[0],
        query_gain.reshape(1, T), key_gain.reshape(1, T),
    )
    eq, eh, ef, gq, gk, gv, qgain, kgain = outs
    return (eq[None], eh[None], ef[None], gq[None], gk[None], gv[None], qgain[0], kgain[0])


def solution(mesh):
    rows = P("dp", "ctx", None)
    in_specs = (rows, rows, rows, P("dp", None), rows, P(), P())
    out_specs = (rows, rows, rows, rows, rows, rows, P(), P())
    return jax.shard_map(body, mesh=mesh, in_specs=in_specs, out_specs=out_specs, check_vma=False)
```

```python
import functools
import math

import jax
import jax.numpy as jnp
from jax import lax
from jax.experimental import pallas as pl
from jax.experimental.pallas import tpu as pltpu
from jax.sharding import PartitionSpec as P

EPS = 1e-06
T = 128
G = 8
R = 4
W = 4096
NX, NZ = 4, 8
C = 1024
SCALE = 1.0 / math.sqrt(T)
LOG2E = 1.4426950408889634
NEG = -1e30
F32, BF16 = jnp.float32, jnp.bfloat16
MESH = pl.DeviceIdType.MESH
LAST = NX * NZ - 1
HALF = NX * NZ // 2
SLOTS = 9
NT = (((1,), (1,)), ((), ()))
TN = (((0,), (0,)), ((), ()))


def iota(shape, dim):
    return lax.broadcasted_iota(jnp.int32, shape, dim)


def dot(a, b, dims=(((1,), (0,)), ((), ()))):
    return lax.dot_general(a, b, dims, preferred_element_type=F32)


def rows_of(start, size):
    return pl.ds(pl.multiple_of(start, 16), size)


def cols_of(start, size):
    return pl.ds(pl.multiple_of(start, 128), size)


def kernel(
    ny, nc,
    q_ref, k_ref, v_ref, len_ref, cot_ref, qg_ref, kg_ref,
    eq_ref, eh_ref, ef_ref, gq_ref, gk_ref, gv_ref, qgain_ref, kgain_ref,
    qv, kv, vv, halo, kn, uk, ik, vw, qn, uq, iq, pr, bias, att, pool, tokc, ga, rows_s, rows_r,
    blk32, blk, cot_a, cot_b, s2, s2b, rx, zs, rz, rb, dss, lows, dos, dqs, dh_s, dh_r, dk_own, dv_own,
    gz, gy, gx,
    l_sem, h_snd, h_rcv, r_snd, r_rcv, cz_snd, cz_rcv, cx_snd, cx_rcv, cb_snd, cb_rcv,
    px_snd, px_rcv, pz_snd, pz_rcv, pb_snd, pb_rcv, d_snd, d_rcv,
    gz_snd, gz_rcv, gy_snd, gy_rcv, gx_snd, gx_rcv,
):
    dp, ctx = lax.axis_index("dp"), lax.axis_index("ctx")
    z, x = ctx // NX, ctx % NX
    y, core = dp // nc, dp % nc
    nxt, prv = (ctx + 1) % (NX * NZ), (ctx + NX * NZ - 1) % (NX * NZ)
    keeps = ctx < HALF
    sends_b = jnp.logical_and(ctx >= HALF, ctx < LAST)

    def at_z(i):
        return (dp, ((z + i) % NZ) * NX + x)

    def at_x(i):
        return (dp, z * NX + (x + i) % NX)

    def at_y(i):
        return (((y + i) % ny) * nc + core, ctx)

    loads = [
        pltpu.make_async_copy(src, dst, l_sem.at[i])
        for i, (src, dst) in enumerate(((k_ref, kv), (v_ref, vv), (q_ref, qv)))
    ]
    for load in loads:
        load.start()

    barrier = pltpu.get_barrier_semaphore()

    def greet(device):
        pl.semaphore_signal(barrier, inc=1, device_id=device, device_id_type=MESH)

    for i in range(1, NZ):
        greet(at_z(i))
    for i in range(1, NX):
        greet(at_x(i))
    for i in range(1, ny):
        greet(at_y(i))
    for j in range(1, nc):
        for i in range(NX):
            greet((y * nc + (core + j) % nc, z * NX + (x + i) % NX))

    @pl.when(x == NX - 1)
    def _():
        greet((dp, nxt))

    @pl.when(x == 0)
    def _():
        greet((dp, prv))

    @pl.when(sends_b)
    def _():
        greet((dp, LAST))

    @pl.when(ctx == LAST)
    def _():
        @pl.loop(HALF, LAST)
        def _(c):
            greet((dp, c))

    count = (NZ - 1) + (NX - 1) + (ny - 1) + NX * (nc - 1)
    edge = jnp.where(jnp.logical_or(x == 0, x == NX - 1), 1, 0)
    far = jnp.where(ctx == LAST, LAST - HALF, jnp.where(sends_b, 1, 0))
    arrivals = count + edge + far

    lens = jnp.broadcast_to(len_ref[...].astype(F32), (T, T))
    ii, jj = iota((T, T), 0), iota((T, T), 1)
    base = (ctx * T).astype(F32)

    def pick(cond, value, axis):
        return jnp.sum(jnp.where(cond, value, 0.0), axis=axis, keepdims=True)

    lens_col = pick(ii == jj, lens, 1)
    ends_col = pick(jj <= ii, lens, 1)
    ends_row = pick(ii <= jj, jnp.broadcast_to(lens_col, (T, T)), 0)
    starts = ends_row - lens[:1]
    ids_col = pick(base + ii.astype(F32) >= ends_row, 1.0, 1)
    key_pos = base - T + iota((T, 3 * T), 1).astype(F32)
    ids_row = jnp.where(key_pos[:1] < 0.0, -1.0, pick(key_pos >= ends_col, 1.0, 0))
    bias[...] = jnp.where(ids_col == ids_row, 0.0, NEG)
    own_row = ids_row[:, T : 2 * T]
    same = jnp.where(ids_col == own_row, 1.0, 0.0).astype(BF16)
    inv_len = 1.0 / pick(ids_col == jj.astype(F32), lens, 1)
    first_id = jnp.min(own_row, axis=1, keepdims=True)
    last_id = jnp.max(own_row, axis=1, keepdims=True)
    with_prv = jnp.where(ids_col == jnp.max(ids_row[:, :T], axis=1, keepdims=True), 1.0, 0.0)
    with_nxt = jnp.where(ids_col == jnp.min(ids_row[:, 2 * T :], axis=1, keepdims=True), 1.0, 0.0)
    r8 = iota((8, T), 0)
    ends8 = jnp.where(
        jnp.logical_or(
            jnp.logical_and(r8 == 0, own_row == first_id), jnp.logical_and(r8 == 1, own_row == last_id)
        ),
        1.0,
        0.0,
    ).astype(BF16)

    for c in range(4):
        blk32[c * 4 : c * 4 + 4, :] = cot_ref[:, c * C : (c + 1) * C]
    high = blk32[...].astype(BF16)
    blk[:16, :] = high
    blk[16:, :] = (blk32[...] - high.astype(F32)).astype(BF16)

    pl.semaphore_wait(barrier, arrivals)

    def remote(src, dst, snd, rcv, device):
        return pltpu.make_async_remote_copy(
            src_ref=src, dst_ref=dst, send_sem=snd, recv_sem=rcv, device_id=device, device_id_type=MESH
        )

    def halo_copy(g, i):
        src = (kv if i < 2 else vv).at[:, cols_of(g * T, T)]
        return remote(src, halo.at[g, i], h_snd.at[g, i], h_rcv.at[g, i], (dp, nxt if i % 2 == 0 else prv))

    loads[0].wait()
    loads[1].wait()

    @pl.loop(0, G)
    def _(g):
        for i in range(4):
            halo_copy(g, i).start()

    def cz_copy(zz):
        return remote(blk, cot_a.at[rows_of((ctx - zz) * 32, 32)], cz_snd.at[zz], cz_rcv.at[ctx - zz], (dp, zz * NX + x))

    def cz_wait(w):
        return remote(blk, cot_a.at[rows_of(w * 32, 32)], cz_snd.at[0], cz_rcv.at[w], at_z(1))

    def cx_copy(w, i):
        own = cot_a.at[rows_of(w * 32, 32)]
        return remote(own, own, cx_snd.at[w, i], cx_rcv.at[w], at_x(i))

    def cb_copy(c):
        return remote(blk, cot_b.at[rows_of((c - HALF) * 32, 32)], cb_snd.at[0], cb_rcv.at[c - HALF], (dp, LAST))

    first_z, last_z = jnp.maximum(ctx - (SLOTS - 1), 0), jnp.minimum(ctx, NZ - 1)
    first_w = (x + NX * NZ - z) % NX

    def each_slot(fn):
        @pl.loop(0, 3)
        def _(j):
            w = first_w + NX * j

            @pl.when(w < SLOTS)
            def _():
                fn(w)

    def each_z(fn):
        @pl.loop(first_z, last_z + 1)
        def _(zz):
            @pl.when(zz != z)
            def _():
                fn(zz)

    @pl.when(keeps)
    def _():
        @pl.when(ctx - z < SLOTS)
        def _():
            cot_a[rows_of((ctx - z) * 32, 32), :] = blk[...]
        each_z(lambda zz: cz_copy(zz).start())

    @pl.when(sends_b)
    def _():
        cb_copy(ctx).start()

    @pl.when(ctx == LAST)
    def _():
        cot_b[(HALF - 1) * 32 : HALF * 32, :] = blk[...]

    q_gain, k_gain = qg_ref[...], kg_ref[...]

    loads[2].wait()

    @pl.loop(0, G)
    def _(g):
        for p in range(R):
            rows = slice(p * T, (p + 1) * T)
            raw = qv[:, cols_of(g * (R * T) + p * T, T)].astype(F32)
            inv = lax.rsqrt(jnp.mean(raw * raw, axis=-1, keepdims=True) + EPS)
            unit = raw * inv
            uq[g, rows, :] = unit
            iq[g, rows, :] = inv
            qn[g, rows, :] = (unit * q_gain).astype(BF16)

    def forward(g):
        for i in range(4):
            halo_copy(g, i).wait_recv()
        cols = cols_of(g * T, T)
        for i, raw in enumerate((halo[g, 0], kv[:, cols], halo[g, 1])):
            raw = raw.astype(F32)
            inv = lax.rsqrt(jnp.mean(raw * raw, axis=-1, keepdims=True) + EPS)
            unit = raw * inv
            uk[g, i * T : (i + 1) * T, :] = unit
            kn[g, i * T : (i + 1) * T, :] = (unit * k_gain).astype(BF16)
            if i == 1:
                ik[g] = inv
        vw[g, :T, :] = halo[g, 2]
        vw[g, T : 2 * T, :] = vv[:, cols]
        vw[g, 2 * T :, :] = halo[g, 3]
        for p in range(R):
            rows = slice(p * T, (p + 1) * T)
            s = dot(qn[g, rows, :], kn[g], NT) * (SCALE * LOG2E) + bias[...]
            powers = jnp.exp2(s - jnp.max(s, axis=-1, keepdims=True))
            probs = powers * (1.0 / jnp.sum(powers, axis=-1, keepdims=True))
            pr[g, rows, :] = probs
            att[:, cols_of(g * (R * T) + p * T, T)] = dot(probs.astype(BF16), vw[g]).astype(BF16)

    @pl.loop(0, G // 2)
    def _(g):
        forward(g)

    def along_x(w):
        @pl.when(z + w != z * NX + x)
        def _():
            cz_wait(w).wait_recv()
        for i in range(1, NX):
            cx_copy(w, i).start()

    each_slot(along_x)

    @pl.loop(G // 2, G)
    def _(g):
        forward(g)

    for c in range(8):
        cols = slice(c * 512, (c + 1) * 512)
        ends = dot(ends8, att[:, cols])
        rows_s[0, :, cols] = ends[0:1]
        rows_s[1, :, cols] = ends[1:2]

    def row_copy(i):
        return remote(rows_s.at[i], rows_r.at[1 - i], r_snd.at[i], r_rcv.at[1 - i], (dp, prv if i == 0 else nxt))

    row_copy(0).start()
    row_copy(1).start()
    for c in range(8):
        cols = slice(c * 512, (c + 1) * 512)
        pool[:, cols] = dot(same, att[:, cols])

    @pl.loop(0, SLOTS)
    def _(w):
        @pl.when((z + w) % NX != x)
        def _():
            cx_copy(w, 1).wait_recv()

    def docs_of(count):
        rr = iota((1, count), 1)
        return ((rr >> 5) * 4 + (rr & 3)).astype(F32), (rr >> 2) & 3

    doc_a, quarter_a = docs_of(SLOTS * 32)
    doc_a = doc_a + (z * 4).astype(F32)
    doc_b, quarter_b = docs_of(HALF * 32)
    doc_b = doc_b + 4.0 * HALF
    for c in range(8):
        cols = slice((c % 2) * 512, (c % 2 + 1) * 512)
        hot = jnp.where(jnp.logical_and(ids_col == doc_a, quarter_a == c // 2), 1.0, 0.0).astype(BF16)
        tokc[:, c * 512 : (c + 1) * 512] = dot(hot, cot_a[:, cols])

    @pl.when(ctx == LAST)
    def _():
        @pl.loop(HALF, LAST)
        def _(c):
            cb_copy(c).wait_recv()
        for c in range(8):
            cols = slice((c % 2) * 512, (c % 2 + 1) * 512)
            hot = jnp.where(jnp.logical_and(ids_col == doc_b, quarter_b == c // 2), 1.0, 0.0).astype(BF16)
            tokc[:, c * 512 : (c + 1) * 512] += dot(hot, cot_b[:, cols])

    row_copy(0).wait_recv()
    row_copy(1).wait_recv()
    norms, inners = [], []
    for c in range(8):
        cols = slice(c * 512, (c + 1) * 512)
        p = (pool[:, cols] + with_prv * rows_r[0, :, cols] + with_nxt * rows_r[1, :, cols]) * inv_len
        pool[:, cols] = p
        norms.append(jnp.sum(p * p, axis=1, keepdims=True))
        inners.append(jnp.sum(p * tokc[:, cols], axis=1, keepdims=True))

    by_quarter = [norms[2 * c] + norms[2 * c + 1] for c in range(4)]
    inner_quarter = [inners[2 * c] + inners[2 * c + 1] for c in range(4)]
    n1 = by_quarter[0]
    n2 = n1 + by_quarter[1]
    n4 = n2 + by_quarter[2] + by_quarter[3]
    d1 = inner_quarter[0]
    d2 = d1 + inner_quarter[1]
    d4 = d2 + inner_quarter[2] + inner_quarter[3]
    i1, i2, i4 = lax.rsqrt(n1 + EPS), lax.rsqrt(n2 + EPS), lax.rsqrt(n4 + EPS)
    b1, b2, b4 = i1 * i1 * i1 * d1, i2 * i2 * i2 * d2, i4 * i4 * i4 * d4
    left = [i1 + i2 + i4, i2 + i4, i4, i4]
    right = [b1 + b2 + b4, b2 + b4, b4, b4]
    for c in range(8):
        cols = slice(c * 512, (c + 1) * 512)
        ga[:, cols] = ((left[c // 2] * tokc[:, cols] - right[c // 2] * pool[:, cols]) * inv_len).astype(BF16)

    def grad_copy(g, i):
        return remote(
            dh_s.at[g, i], dh_r.at[g, i], d_snd.at[g, i], d_rcv.at[g, i], (dp, prv if i % 2 == 0 else nxt)
        )

    def scores(g, carry):
        q_sum, k_sum = carry
        for p in range(R):
            rows = slice(p * T, (p + 1) * T)
            probs = pr[g, rows, :]
            dprobs = dot(ga[:, cols_of(g * (R * T) + p * T, T)], vw[g], NT)
            inner = jnp.sum(probs * dprobs, axis=-1, keepdims=True)
            ds = (probs * (dprobs - inner)).astype(BF16)
            dss[rows, :] = ds
            dq = dot(ds, kn[g]) * SCALE
            dqs[g, rows, :] = dq
            q_sum = q_sum + jnp.sum(dq * uq[g, rows, :], axis=0, keepdims=True)
        dk = dot(dss[...], qn[g], TN) * SCALE
        k_sum = k_sum + jnp.sum(dk * uk[g], axis=0, keepdims=True)
        dh_s[g, 0] = dk[:T].astype(BF16)
        dh_s[g, 1] = dk[2 * T :].astype(BF16)
        for i in range(2):
            grad_copy(g, i).start()
        dk_own[g] = dk[T : 2 * T]
        return q_sum, k_sum

    def finish(g):
        for p in range(R):
            cols = cols_of(g * (R * T) + p * T, T)
            rows = slice(p * T, (p + 1) * T)
            dos[rows, :] = ga[:, cols]
            lows[rows, :] = pr[g, rows, :].astype(BF16)
            unit = uq[g, rows, :]
            scaled = dqs[g, rows, :] * q_gain
            mean = jnp.mean(scaled * unit, axis=-1, keepdims=True)
            gq_ref[:, cols] = (iq[g, rows, :] * (scaled - unit * mean)).astype(BF16)
        dv = dot(lows[...], dos[...], TN)
        dh_s[g, 2] = dv[:T].astype(BF16)
        dh_s[g, 3] = dv[2 * T :].astype(BF16)
        for i in range(2, 4):
            grad_copy(g, i).start()
        dv_own[g] = dv[T : 2 * T]

    zero = jnp.zeros((1, T), F32)
    sums = lax.fori_loop(0, G // 2, scores, (zero, zero))

    def gathered(count, first):
        rc, tc = iota((count * 16, T), 0), iota((count * 16, T), 1)
        doc_of = first + (rc >> 4) * 4 + (rc & 3)
        here = pick(doc_of == tc, starts, 1) - base == tc.astype(F32)
        part = (rc >> 2) & 3
        hots = [jnp.where(jnp.logical_and(here, part == c), 1.0, 0.0).astype(BF16) for c in range(4)]
        halves = []
        for h in range(2):
            total = None
            for c in range(4):
                term = dot(hots[c], pool[:, c * C + h * 512 : c * C + (h + 1) * 512].astype(BF16))
                total = term if total is None else total + term
            halves.append(total.astype(BF16))
        return halves

    halves = gathered(SLOTS, z * 4)
    for h in range(2):
        s2[:, h * 512 : (h + 1) * 512] = halves[h]

    def px_copy(w):
        dst = rx.at[x, rows_of((w // NX) * 16, 16)]
        return remote(s2.at[rows_of(w * 16, 16)], dst, px_snd.at[w], px_rcv.at[x, w // NX], (dp, z * NX + (z + w) % NX))

    def px_wait(w, xx):
        dst = rx.at[xx, rows_of((w // NX) * 16, 16)]
        return remote(s2.at[rows_of(0, 16)], dst, px_snd.at[0], px_rcv.at[xx, w // NX], at_x(1))

    def other_slots(fn):
        @pl.loop(0, SLOTS)
        def _(w):
            @pl.when((z + w) % NX != x)
            def _():
                fn(w)

    other_slots(lambda w: px_copy(w).start())

    def pb_copy(c):
        return remote(s2b.at[rows_of((c - HALF) * 16, 16)], rb, pb_snd.at[c - HALF], pb_rcv.at[0], (dp, c))

    @pl.when(ctx == LAST)
    def _():
        halves = gathered(HALF, 4 * HALF)
        for h in range(2):
            s2b[:, h * 512 : (h + 1) * 512] = halves[h]

        @pl.loop(HALF, LAST)
        def _(c):
            pb_copy(c).start()

    q_sum, k_sum = lax.fori_loop(G // 2, G, scores, sums)

    def total_of(slots, count, copies):
        for copy in copies:
            copy[1].wait_recv()
        total = slots[0]
        for i in range(1, count):
            total = total + slots[i]
        return total

    def send(copies):
        for copy in copies:
            copy[0].start()

    def gain_pair(slots, snd, rcv, i, place, other, device):
        return (
            remote(slots.at[place], slots.at[place], snd.at[i], rcv.at[place], device),
            remote(slots.at[other], slots.at[other], snd.at[i], rcv.at[other], device),
        )

    r8 = iota((8, T), 0)
    gz[z] = jnp.where(r8 == 0, q_sum, jnp.where(r8 == 1, k_sum, 0.0))
    z_pairs = [gain_pair(gz, gz_snd, gz_rcv, i, z, (z + i) % NZ, at_z(i)) for i in range(1, NZ)]
    y_pairs = [gain_pair(gy, gy_snd, gy_rcv, i, y, (y + i) % ny, at_y(i)) for i in range(1, ny)]
    spot = core * NX + x
    x_pairs = []
    for j in range(nc):
        for i in range(NX):
            if i or j:
                there = (core + j) % nc
                other = there * NX + (x + i) % NX
                device = (y * nc + there, z * NX + (x + i) % NX)
                x_pairs.append(gain_pair(gx, gx_snd, gx_rcv, j * NX + i, spot, other, device))
    send(z_pairs)

    def pz_copy(w):
        src = zs.at[rows_of((w // NX) * 16, 16)]
        return remote(src, rz.at[z], pz_snd.at[w // NX], pz_rcv.at[z], (dp, z + w))

    def pz_wait(zz):
        return remote(zs.at[rows_of(0, 16)], rz.at[zz], pz_snd.at[0], pz_rcv.at[zz], at_z(1))

    def merge(w):
        rows = s2[rows_of(w * 16, 16), :].astype(F32)
        for i in range(1, NX):
            xx = (x + i) % NX
            px_wait(w, xx).wait_recv()
            rows = rows + rx[xx, rows_of((w // NX) * 16, 16), :].astype(F32)
        zs[rows_of((w // NX) * 16, 16), :] = rows.astype(BF16)

        @pl.when(z + w != ctx)
        def _():
            pz_copy(w).start()

    each_slot(merge)

    @pl.loop(0, G // 2)
    def _(g):
        finish(g)

    gy[y] = total_of(gz, NZ, z_pairs)
    send(y_pairs)

    @pl.loop(G // 2, G)
    def _(g):
        finish(g)

    gx[spot] = total_of(gy, ny, y_pairs)
    send(x_pairs)

    @pl.loop(0, G)
    def _(g):
        for i in range(4):
            grad_copy(g, i).wait_recv()
        cols = cols_of(g * T, T)
        dk = dk_own[g] + (dh_r[g, 0].astype(F32) + dh_r[g, 1].astype(F32))
        dv = dv_own[g] + (dh_r[g, 2].astype(F32) + dh_r[g, 3].astype(F32))
        unit = uk[g, T : 2 * T, :]
        scaled = dk * k_gain
        mean = jnp.mean(scaled * unit, axis=-1, keepdims=True)
        gk_ref[:, cols] = (ik[g] * (scaled - unit * mean)).astype(BF16)
        gv_ref[:, cols] = dv.astype(BF16)

    def embed(rows):
        parts = [rows[c * 4 : c * 4 + 4] for c in range(4)]
        squares = [jnp.sum(part * part, axis=1, keepdims=True) for part in parts]
        m1 = squares[0]
        m2 = m1 + squares[1]
        m4 = m2 + squares[2] + squares[3]
        eq_ref[...] = parts[0] * lax.rsqrt(m1 + EPS)
        for ref, m, count in ((eh_ref, m2, 2), (ef_ref, m4, 4)):
            inv = lax.rsqrt(m + EPS)
            for c in range(count):
                ref[:, c * C : (c + 1) * C] = parts[c] * inv

    @pl.when(keeps)
    def _():
        near = ctx - z < SLOTS
        blk32[...] = jnp.zeros_like(blk32)

        @pl.when(near)
        def _():
            blk32[...] = zs[rows_of(((ctx - z) // NX) * 16 % 48, 16), :].astype(F32)

        @pl.loop(first_z, last_z + 1)
        def _(zz):
            @pl.when(zz != z)
            def _():
                pz_wait(zz).wait_recv()
                blk32[...] += rz[zz].astype(F32)
        embed(blk32[...])

    @pl.when(sends_b)
    def _():
        pb_copy(ctx).wait_recv()
        embed(rb[...].astype(F32))

    @pl.when(ctx == LAST)
    def _():
        embed(s2b[(HALF - 1) * 16 : HALF * 16, :].astype(F32))

    total = total_of(gx, NX * nc, x_pairs)
    qgain_ref[...] = total[0:1]
    kgain_ref[...] = total[1:2]

    @pl.loop(0, G)
    def _(g):
        for i in range(4):
            halo_copy(g, i).wait_send()
            grad_copy(g, i).wait_send()
    row_copy(0).wait_send()
    row_copy(1).wait_send()

    def sent(w):
        for i in range(1, NX):
            cx_copy(w, i).wait_send()

        @pl.when(z + w != ctx)
        def _():
            pz_copy(w).wait_send()

    each_slot(sent)
    other_slots(lambda w: px_copy(w).wait_send())

    @pl.when(keeps)
    def _():
        each_z(lambda zz: cz_copy(zz).wait_send())

    @pl.when(sends_b)
    def _():
        cb_copy(ctx).wait_send()

    @pl.when(ctx == LAST)
    def _():
        @pl.loop(HALF, LAST)
        def _(c):
            pb_copy(c).wait_send()
    for pair in z_pairs + y_pairs + x_pairs:
        pair[0].wait_send()


def emit(*refs):
    srcs, dsts, held, sem = refs[:8], refs[8:16], refs[16:24], refs[24]
    moves = []
    for i in range(8):
        parts = 4 if i == 3 else 1
        size = srcs[i].shape[0] // parts
        for p in range(parts):
            at = pl.ds(p * size, size)
            n = len(moves)
            first = pltpu.make_async_copy(srcs[i].at[at], held[i].at[at], sem.at[0, n])
            moves.append((first, pltpu.make_async_copy(held[i].at[at], dsts[i].at[at], sem.at[1, n])))
    order = sorted(range(len(moves)), key=lambda n: not 3 <= n < 7)
    for n in order:
        moves[n][0].start()
    for n in order:
        moves[n][0].wait()
        moves[n][1].start()
    for n in order:
        moves[n][1].wait()


def body(queries, keys, values, doc_lengths, cotangent, query_gain, key_gain):
    nc = 2 if lax.axis_size("dp") > 1 else 1
    ny = lax.axis_size("dp") // nc
    vmem, dma = pltpu.VMEM, pltpu.SemaphoreType.DMA
    scratch = [
        vmem((T, W), BF16),
        vmem((T, G * T), BF16),
        vmem((T, G * T), BF16),
        vmem((G, 4, T, T), BF16),
        vmem((G, 3 * T, T), BF16),
        vmem((G, 3 * T, T), F32),
        vmem((G, T, 1), F32),
        vmem((G, 3 * T, T), BF16),
        vmem((G, R * T, T), BF16),
        vmem((G, R * T, T), F32),
        vmem((G, R * T, 1), F32),
        vmem((G, R * T, 3 * T), F32),
        vmem((T, 3 * T), F32),
        vmem((T, W), BF16),
        vmem((T, W), F32),
        vmem((T, W), F32),
        vmem((T, W), BF16),
        vmem((2, 1, W), F32),
        vmem((2, 1, W), F32),
        vmem((16, C), F32),
        vmem((32, C), BF16),
        vmem((SLOTS * 32, C), BF16),
        vmem((HALF * 32, C), BF16),
        vmem((SLOTS * 16, C), BF16),
        vmem((HALF * 16, C), BF16),
        vmem((NX, 48, C), BF16),
        vmem((48, C), BF16),
        vmem((NZ, 16, C), BF16),
        vmem((16, C), BF16),
        vmem((R * T, 3 * T), BF16),
        vmem((R * T, 3 * T), BF16),
        vmem((R * T, T), BF16),
        vmem((G, R * T, T), F32),
        vmem((G, 4, T, T), BF16),
        vmem((G, 4, T, T), BF16),
        vmem((G, T, T), F32),
        vmem((G, T, T), F32),
        vmem((NZ, 8, T), F32),
        vmem((ny, 8, T), F32),
        vmem((nc * NX, 8, T), F32),
        dma((3,)),
        dma((G, 4)), dma((G, 4)),
        dma((2,)), dma((2,)),
        dma((NZ,)), dma((SLOTS,)),
        dma((SLOTS, NX)), dma((SLOTS,)),
        dma((1,)), dma((HALF,)),
        dma((SLOTS,)), dma((NX, 3)),
        dma((3,)), dma((NZ,)),
        dma((HALF,)), dma((1,)),
        dma((G, 4)), dma((G, 4)),
        dma((NZ,)), dma((NZ,)),
        dma((ny,)), dma((ny,)),
        dma((nc * NX,)), dma((nc * NX,)),
    ]
    shape = jax.ShapeDtypeStruct
    outs = pl.pallas_call(
        functools.partial(kernel, ny, nc),
        out_shape=(
            shape((4, C), F32),
            shape((4, 2 * C), F32),
            shape((4, W), F32),
            shape((T, W), BF16),
            shape((T, G * T), BF16),
            shape((T, G * T), BF16),
            shape((1, T), F32),
            shape((1, T), F32),
        ),
        in_specs=[pl.BlockSpec(memory_space=pl.ANY)] * 3 + [pl.BlockSpec(memory_space=pltpu.VMEM)] * 4,
        out_specs=tuple([pl.BlockSpec(memory_space=pltpu.VMEM)] * 8),
        scratch_shapes=scratch,
        compiler_params=pltpu.CompilerParams(
            collective_id=0, has_side_effects=True, vmem_limit_bytes=56 * 1024 * 1024
        ),
    )(
        queries[0], keys[0], values[0], doc_lengths, cotangent[0],
        query_gain.reshape(1, T), key_gain.reshape(1, T),
    )
    outs = pl.pallas_call(
        emit,
        out_shape=tuple(shape(out.shape, out.dtype) for out in outs),
        in_specs=[pl.BlockSpec(memory_space=pl.ANY)] * 8,
        out_specs=tuple([pl.BlockSpec(memory_space=pl.ANY)] * 8),
        scratch_shapes=[vmem(out.shape, out.dtype) for out in outs] + [dma((2, 11))],
    )(*outs)
    eq, eh, ef, gq, gk, gv, qgain, kgain = outs
    return (eq[None], eh[None], ef[None], gq[None], gk[None], gv[None], qgain[0], kgain[0])


def solution(mesh):
    rows = P("dp", "ctx", None)
    in_specs = (rows, rows, rows, P("dp", None), rows, P(), P())
    out_specs = (rows, rows, rows, rows, rows, rows, P(), P())
    return jax.shard_map(body, mesh=mesh, in_specs=in_specs, out_specs=out_specs, check_vma=False)
```

```python
import functools
import math

import jax
import jax.numpy as jnp
from jax import lax
from jax.experimental import pallas as pl
from jax.experimental.pallas import tpu as pltpu
from jax.sharding import PartitionSpec as P

EPS = 1e-06
T = 128
G = 8
R = 4
W = 4096
NX, NZ = 4, 8
C = 1024
SCALE = 1.0 / math.sqrt(T)
LOG2E = 1.4426950408889634
NEG = -1e30
F32, BF16 = jnp.float32, jnp.bfloat16
MESH = pl.DeviceIdType.MESH
LAST = NX * NZ - 1
HALF = NX * NZ // 2
SLOTS = 9
NT = (((1,), (1,)), ((), ()))
TN = (((0,), (0,)), ((), ()))


def iota(shape, dim):
    return lax.broadcasted_iota(jnp.int32, shape, dim)


def dot(a, b, dims=(((1,), (0,)), ((), ()))):
    return lax.dot_general(a, b, dims, preferred_element_type=F32)


def rows_of(start, size):
    return pl.ds(pl.multiple_of(start, 16), size)


def cols_of(start, size):
    return pl.ds(pl.multiple_of(start, 128), size)


def kernel(
    ny, nc,
    q_ref, k_ref, v_ref, len_ref, cot_ref, qg_ref, kg_ref,
    eq_ref, eh_ref, ef_ref, gq_ref, gk_ref, gv_ref, qgain_ref, kgain_ref,
    qv, kv, vv, halo, kn, uk, ik, vw, qn, uq, iq, pr, bias, att, pool, tokc, ga, rows_s, rows_r,
    blk32, blk, cot_a, cot_b, s2, s2b, rx, zs, rz, rb, dss, lows, dos, dqs, dh_s, dh_r, dk_own, dv_own,
    gz, gy, gx,
    l_sem, h_snd, h_rcv, r_snd, r_rcv, cz_snd, cz_rcv, cx_snd, cx_rcv, cb_snd, cb_rcv,
    px_snd, px_rcv, pz_snd, pz_rcv, pb_snd, pb_rcv, d_snd, d_rcv,
    gz_snd, gz_rcv, gy_snd, gy_rcv, gx_snd, gx_rcv,
):
    dp, ctx = lax.axis_index("dp"), lax.axis_index("ctx")
    z, x = ctx // NX, ctx % NX
    y, core = dp // nc, dp % nc
    nxt, prv = (ctx + 1) % (NX * NZ), (ctx + NX * NZ - 1) % (NX * NZ)
    keeps = ctx < HALF
    sends_b = jnp.logical_and(ctx >= HALF, ctx < LAST)

    def at_z(i):
        return (dp, ((z + i) % NZ) * NX + x)

    def at_x(i):
        return (dp, z * NX + (x + i) % NX)

    def at_y(i):
        return (((y + i) % ny) * nc + core, ctx)

    loads = [
        pltpu.make_async_copy(src, dst, l_sem.at[i])
        for i, (src, dst) in enumerate(((k_ref, kv), (v_ref, vv), (q_ref, qv)))
    ]
    for load in loads:
        load.start()

    barrier = pltpu.get_barrier_semaphore()

    def greet(device):
        pl.semaphore_signal(barrier, inc=1, device_id=device, device_id_type=MESH)

    for i in range(1, NZ):
        greet(at_z(i))
    for i in range(1, NX):
        greet(at_x(i))
    for i in range(1, ny):
        greet(at_y(i))
    for j in range(1, nc):
        for i in range(NX):
            greet((y * nc + (core + j) % nc, z * NX + (x + i) % NX))

    @pl.when(x == NX - 1)
    def _():
        greet((dp, nxt))

    @pl.when(x == 0)
    def _():
        greet((dp, prv))

    @pl.when(sends_b)
    def _():
        greet((dp, LAST))

    @pl.when(ctx == LAST)
    def _():
        @pl.loop(HALF, LAST)
        def _(c):
            greet((dp, c))

    count = (NZ - 1) + (NX - 1) + (ny - 1) + NX * (nc - 1)
    edge = jnp.where(jnp.logical_or(x == 0, x == NX - 1), 1, 0)
    far = jnp.where(ctx == LAST, LAST - HALF, jnp.where(sends_b, 1, 0))
    arrivals = count + edge + far

    lens = jnp.broadcast_to(len_ref[...].astype(F32), (T, T))
    ii, jj = iota((T, T), 0), iota((T, T), 1)
    base = (ctx * T).astype(F32)

    def pick(cond, value, axis):
        return jnp.sum(jnp.where(cond, value, 0.0), axis=axis, keepdims=True)

    lens_col = pick(ii == jj, lens, 1)
    ends_col = pick(jj <= ii, lens, 1)
    ends_row = pick(ii <= jj, jnp.broadcast_to(lens_col, (T, T)), 0)
    starts = ends_row - lens[:1]
    ids_col = pick(base + ii.astype(F32) >= ends_row, 1.0, 1)
    key_pos = base - T + iota((T, 3 * T), 1).astype(F32)
    ids_row = jnp.where(key_pos[:1] < 0.0, -1.0, pick(key_pos >= ends_col, 1.0, 0))
    bias[...] = jnp.where(ids_col == ids_row, 0.0, NEG)
    own_row = ids_row[:, T : 2 * T]
    same = jnp.where(ids_col == own_row, 1.0, 0.0).astype(BF16)
    inv_len = 1.0 / pick(ids_col == jj.astype(F32), lens, 1)
    with_prv = jnp.where(ids_col == jnp.max(ids_row[:, :T], axis=1, keepdims=True), 1.0, 0.0)
    with_nxt = jnp.where(ids_col == jnp.min(ids_row[:, 2 * T :], axis=1, keepdims=True), 1.0, 0.0)

    for c in range(4):
        blk32[c * 4 : c * 4 + 4, :] = cot_ref[:, c * C : (c + 1) * C]
    high = blk32[...].astype(BF16)
    blk[:16, :] = high
    blk[16:, :] = (blk32[...] - high.astype(F32)).astype(BF16)

    pl.semaphore_wait(barrier, arrivals)

    def remote(src, dst, snd, rcv, device):
        return pltpu.make_async_remote_copy(
            src_ref=src, dst_ref=dst, send_sem=snd, recv_sem=rcv, device_id=device, device_id_type=MESH
        )

    def halo_copy(g, i):
        src = (kv if i < 2 else vv).at[:, cols_of(g * T, T)]
        return remote(src, halo.at[g, i], h_snd.at[g, i], h_rcv.at[g, i], (dp, nxt if i % 2 == 0 else prv))

    loads[0].wait()
    loads[1].wait()

    @pl.loop(0, G)
    def _(g):
        for i in range(4):
            halo_copy(g, i).start()

    def cz_copy(zz):
        return remote(blk, cot_a.at[rows_of((ctx - zz) * 32, 32)], cz_snd.at[zz], cz_rcv.at[ctx - zz], (dp, zz * NX + x))

    def cz_wait(w):
        return remote(blk, cot_a.at[rows_of(w * 32, 32)], cz_snd.at[0], cz_rcv.at[w], at_z(1))

    def cx_copy(w, i):
        own = cot_a.at[rows_of(w * 32, 32)]
        return remote(own, own, cx_snd.at[w, i], cx_rcv.at[w], at_x(i))

    def cb_copy(c):
        return remote(blk, cot_b.at[rows_of((c - HALF) * 32, 32)], cb_snd.at[0], cb_rcv.at[c - HALF], (dp, LAST))

    first_z, last_z = jnp.maximum(ctx - (SLOTS - 1), 0), jnp.minimum(ctx, NZ - 1)
    first_w = (x + NX * NZ - z) % NX

    def each_slot(fn):
        @pl.loop(0, 3)
        def _(j):
            w = first_w + NX * j

            @pl.when(w < SLOTS)
            def _():
                fn(w)

    def each_z(fn):
        @pl.loop(first_z, last_z + 1)
        def _(zz):
            @pl.when(zz != z)
            def _():
                fn(zz)

    @pl.when(keeps)
    def _():
        @pl.when(ctx - z < SLOTS)
        def _():
            cot_a[rows_of((ctx - z) * 32, 32), :] = blk[...]
        each_z(lambda zz: cz_copy(zz).start())

    @pl.when(sends_b)
    def _():
        cb_copy(ctx).start()

    @pl.when(ctx == LAST)
    def _():
        cot_b[(HALF - 1) * 32 : HALF * 32, :] = blk[...]

    q_gain, k_gain = qg_ref[...], kg_ref[...]

    loads[2].wait()

    @pl.loop(0, G)
    def _(g):
        for p in range(R):
            rows = slice(p * T, (p + 1) * T)
            raw = qv[:, cols_of(g * (R * T) + p * T, T)].astype(F32)
            inv = lax.rsqrt(jnp.mean(raw * raw, axis=-1, keepdims=True) + EPS)
            unit = raw * inv
            uq[g, rows, :] = unit
            iq[g, rows, :] = inv
            qn[g, rows, :] = (unit * q_gain).astype(BF16)

    def forward(g):
        for i in range(4):
            halo_copy(g, i).wait_recv()
        cols = cols_of(g * T, T)
        for i, raw in enumerate((halo[g, 0], kv[:, cols], halo[g, 1])):
            raw = raw.astype(F32)
            inv = lax.rsqrt(jnp.mean(raw * raw, axis=-1, keepdims=True) + EPS)
            unit = raw * inv
            uk[g, i * T : (i + 1) * T, :] = unit
            kn[g, i * T : (i + 1) * T, :] = (unit * k_gain).astype(BF16)
            if i == 1:
                ik[g] = inv
        vw[g, :T, :] = halo[g, 2]
        vw[g, T : 2 * T, :] = vv[:, cols]
        vw[g, 2 * T :, :] = halo[g, 3]
        products = dot(qn[g], kn[g], NT)
        for p in range(R):
            rows = slice(p * T, (p + 1) * T)
            s = products[rows] * (SCALE * LOG2E) + bias[...]
            powers = jnp.exp2(s - jnp.max(s, axis=-1, keepdims=True))
            probs = powers * (1.0 / jnp.sum(powers, axis=-1, keepdims=True))
            pr[g, rows, :] = probs
            lows[g, rows, :] = probs.astype(BF16)
        mixed = dot(lows[g], vw[g]).astype(BF16)
        for p in range(R):
            att[:, cols_of(g * (R * T) + p * T, T)] = mixed[p * T : (p + 1) * T]

    @pl.loop(0, G // 2)
    def _(g):
        forward(g)

    def along_x(w):
        @pl.when(z + w != z * NX + x)
        def _():
            cz_wait(w).wait_recv()
        for i in range(1, NX):
            cx_copy(w, i).start()

    each_slot(along_x)

    @pl.loop(G // 2, G)
    def _(g):
        forward(g)

    for c in range(8):
        cols = slice(c * 512, (c + 1) * 512)
        sums = dot(same, att[:, cols])
        pool[:, cols] = sums
        rows_s[0, :, cols] = sums[:1]
        rows_s[1, :, cols] = sums[T - 1 :]

    def row_copy(i):
        return remote(rows_s.at[i], rows_r.at[1 - i], r_snd.at[i], r_rcv.at[1 - i], (dp, prv if i == 0 else nxt))

    row_copy(0).start()
    row_copy(1).start()
    @pl.loop(0, SLOTS)
    def _(w):
        @pl.when((z + w) % NX != x)
        def _():
            cx_copy(w, 1).wait_recv()

    def docs_of(count):
        rr = iota((1, count), 1)
        return ((rr >> 5) * 4 + (rr & 3)).astype(F32), (rr >> 2) & 3

    doc_a, quarter_a = docs_of(SLOTS * 32)
    doc_a = doc_a + (z * 4).astype(F32)
    doc_b, quarter_b = docs_of(HALF * 32)
    doc_b = doc_b + 4.0 * HALF
    def spread(doc, quarter, blocks, add):
        hits = ids_col == doc
        hot = jnp.concatenate(
            [jnp.where(jnp.logical_and(hits, quarter == c), 1.0, 0.0).astype(BF16) for c in range(4)], axis=0
        )
        for h in range(4):
            term = dot(hot, blocks[:, h * 256 : (h + 1) * 256])
            for c in range(4):
                cols = slice(c * C + h * 256, c * C + (h + 1) * 256)
                rows = term[c * T : (c + 1) * T]
                tokc[:, cols] = tokc[:, cols] + rows if add else rows

    spread(doc_a, quarter_a, cot_a, False)

    @pl.when(ctx == LAST)
    def _():
        @pl.loop(HALF, LAST)
        def _(c):
            cb_copy(c).wait_recv()
        spread(doc_b, quarter_b, cot_b, True)

    row_copy(0).wait_recv()
    row_copy(1).wait_recv()
    norms, inners = [], []
    for c in range(8):
        cols = slice(c * 512, (c + 1) * 512)
        p = (pool[:, cols] + with_prv * rows_r[0, :, cols] + with_nxt * rows_r[1, :, cols]) * inv_len
        pool[:, cols] = p
        norms.append(jnp.sum(p * p, axis=1, keepdims=True))
        inners.append(jnp.sum(p * tokc[:, cols], axis=1, keepdims=True))

    by_quarter = [norms[2 * c] + norms[2 * c + 1] for c in range(4)]
    inner_quarter = [inners[2 * c] + inners[2 * c + 1] for c in range(4)]
    n1 = by_quarter[0]
    n2 = n1 + by_quarter[1]
    n4 = n2 + by_quarter[2] + by_quarter[3]
    d1 = inner_quarter[0]
    d2 = d1 + inner_quarter[1]
    d4 = d2 + inner_quarter[2] + inner_quarter[3]
    i1, i2, i4 = lax.rsqrt(n1 + EPS), lax.rsqrt(n2 + EPS), lax.rsqrt(n4 + EPS)
    b1, b2, b4 = i1 * i1 * i1 * d1, i2 * i2 * i2 * d2, i4 * i4 * i4 * d4
    left = [i1 + i2 + i4, i2 + i4, i4, i4]
    right = [b1 + b2 + b4, b2 + b4, b4, b4]
    for c in range(8):
        cols = slice(c * 512, (c + 1) * 512)
        ga[:, cols] = ((left[c // 2] * tokc[:, cols] - right[c // 2] * pool[:, cols]) * inv_len).astype(BF16)

    def grad_copy(g, i):
        return remote(
            dh_s.at[g, i], dh_r.at[g, i], d_snd.at[g, i], d_rcv.at[g, i], (dp, prv if i % 2 == 0 else nxt)
        )

    def scores(g, carry):
        q_sum, k_sum = carry
        for p in range(R):
            dos[p * T : (p + 1) * T, :] = ga[:, cols_of(g * (R * T) + p * T, T)]
        products = dot(dos[...], vw[g], NT)
        for p in range(R):
            rows = slice(p * T, (p + 1) * T)
            probs, dprobs = pr[g, rows, :], products[rows]
            inner = jnp.sum(probs * dprobs, axis=-1, keepdims=True)
            dss[rows, :] = (probs * (dprobs - inner)).astype(BF16)
        dq = dot(dss[...], kn[g]) * SCALE
        dqs[g] = dq
        q_sum = q_sum + jnp.sum(dq * uq[g], axis=0, keepdims=True)
        dk = dot(dss[...], qn[g], TN) * SCALE
        k_sum = k_sum + jnp.sum(dk * uk[g], axis=0, keepdims=True)
        dh_s[g, 0] = dk[:T].astype(BF16)
        dh_s[g, 1] = dk[2 * T :].astype(BF16)
        for i in range(2):
            grad_copy(g, i).start()
        dk_own[g] = dk[T : 2 * T]
        return q_sum, k_sum

    def finish(g):
        for p in range(R):
            cols = cols_of(g * (R * T) + p * T, T)
            rows = slice(p * T, (p + 1) * T)
            dos[rows, :] = ga[:, cols]
            unit = uq[g, rows, :]
            scaled = dqs[g, rows, :] * q_gain
            mean = jnp.mean(scaled * unit, axis=-1, keepdims=True)
            gq_ref[:, cols] = (iq[g, rows, :] * (scaled - unit * mean)).astype(BF16)
        dv = dot(lows[g], dos[...], TN)
        dh_s[g, 2] = dv[:T].astype(BF16)
        dh_s[g, 3] = dv[2 * T :].astype(BF16)
        for i in range(2, 4):
            grad_copy(g, i).start()
        dv_own[g] = dv[T : 2 * T]

    zero = jnp.zeros((1, T), F32)
    sums = lax.fori_loop(0, G // 2, scores, (zero, zero))

    def gathered(count, first):
        rc, tc = iota((count * 16, T), 0), iota((count * 16, T), 1)
        doc_of = first + (rc >> 4) * 4 + (rc & 3)
        here = pick(doc_of == tc, starts, 1) - base == tc.astype(F32)
        part = (rc >> 2) & 3
        hots = [jnp.where(jnp.logical_and(here, part == c), 1.0, 0.0).astype(BF16) for c in range(4)]
        halves = []
        for h in range(2):
            total = None
            for c in range(4):
                term = dot(hots[c], pool[:, c * C + h * 512 : c * C + (h + 1) * 512].astype(BF16))
                total = term if total is None else total + term
            halves.append(total.astype(BF16))
        return halves

    halves = gathered(SLOTS, z * 4)
    for h in range(2):
        s2[:, h * 512 : (h + 1) * 512] = halves[h]

    def px_copy(w):
        dst = rx.at[x, rows_of((w // NX) * 16, 16)]
        return remote(s2.at[rows_of(w * 16, 16)], dst, px_snd.at[w], px_rcv.at[x, w // NX], (dp, z * NX + (z + w) % NX))

    def px_wait(w, xx):
        dst = rx.at[xx, rows_of((w // NX) * 16, 16)]
        return remote(s2.at[rows_of(0, 16)], dst, px_snd.at[0], px_rcv.at[xx, w // NX], at_x(1))

    def other_slots(fn):
        @pl.loop(0, SLOTS)
        def _(w):
            @pl.when((z + w) % NX != x)
            def _():
                fn(w)

    other_slots(lambda w: px_copy(w).start())

    def pb_copy(c):
        return remote(s2b.at[rows_of((c - HALF) * 16, 16)], rb, pb_snd.at[c - HALF], pb_rcv.at[0], (dp, c))

    @pl.when(ctx == LAST)
    def _():
        halves = gathered(HALF, 4 * HALF)
        for h in range(2):
            s2b[:, h * 512 : (h + 1) * 512] = halves[h]

        @pl.loop(HALF, LAST)
        def _(c):
            pb_copy(c).start()

    q_sum, k_sum = lax.fori_loop(G // 2, G, scores, sums)

    def total_of(slots, count, copies):
        for copy in copies:
            copy[1].wait_recv()
        total = slots[0]
        for i in range(1, count):
            total = total + slots[i]
        return total

    def send(copies):
        for copy in copies:
            copy[0].start()

    def gain_pair(slots, snd, rcv, i, place, other, device):
        return (
            remote(slots.at[place], slots.at[place], snd.at[i], rcv.at[place], device),
            remote(slots.at[other], slots.at[other], snd.at[i], rcv.at[other], device),
        )

    r8 = iota((8, T), 0)
    gz[z] = jnp.where(r8 == 0, q_sum, jnp.where(r8 == 1, k_sum, 0.0))
    z_pairs = [gain_pair(gz, gz_snd, gz_rcv, i, z, (z + i) % NZ, at_z(i)) for i in range(1, NZ)]
    y_pairs = [gain_pair(gy, gy_snd, gy_rcv, i, y, (y + i) % ny, at_y(i)) for i in range(1, ny)]
    spot = core * NX + x
    x_pairs = []
    for j in range(nc):
        for i in range(NX):
            if i or j:
                there = (core + j) % nc
                other = there * NX + (x + i) % NX
                device = (y * nc + there, z * NX + (x + i) % NX)
                x_pairs.append(gain_pair(gx, gx_snd, gx_rcv, j * NX + i, spot, other, device))
    send(z_pairs)

    def pz_copy(w):
        src = zs.at[rows_of((w // NX) * 16, 16)]
        return remote(src, rz.at[z], pz_snd.at[w // NX], pz_rcv.at[z], (dp, z + w))

    def pz_wait(zz):
        return remote(zs.at[rows_of(0, 16)], rz.at[zz], pz_snd.at[0], pz_rcv.at[zz], at_z(1))

    def merge(w):
        rows = s2[rows_of(w * 16, 16), :].astype(F32)
        for i in range(1, NX):
            xx = (x + i) % NX
            px_wait(w, xx).wait_recv()
            rows = rows + rx[xx, rows_of((w // NX) * 16, 16), :].astype(F32)
        zs[rows_of((w // NX) * 16, 16), :] = rows.astype(BF16)

        @pl.when(z + w != ctx)
        def _():
            pz_copy(w).start()

    each_slot(merge)

    @pl.loop(0, G // 2)
    def _(g):
        finish(g)

    gy[y] = total_of(gz, NZ, z_pairs)
    send(y_pairs)

    @pl.loop(G // 2, G)
    def _(g):
        finish(g)

    gx[spot] = total_of(gy, ny, y_pairs)
    send(x_pairs)

    @pl.loop(0, G)
    def _(g):
        for i in range(4):
            grad_copy(g, i).wait_recv()
        cols = cols_of(g * T, T)
        dk = dk_own[g] + (dh_r[g, 0].astype(F32) + dh_r[g, 1].astype(F32))
        dv = dv_own[g] + (dh_r[g, 2].astype(F32) + dh_r[g, 3].astype(F32))
        unit = uk[g, T : 2 * T, :]
        scaled = dk * k_gain
        mean = jnp.mean(scaled * unit, axis=-1, keepdims=True)
        gk_ref[:, cols] = (ik[g] * (scaled - unit * mean)).astype(BF16)
        gv_ref[:, cols] = dv.astype(BF16)

    def embed(rows):
        parts = [rows[c * 4 : c * 4 + 4] for c in range(4)]
        squares = [jnp.sum(part * part, axis=1, keepdims=True) for part in parts]
        m1 = squares[0]
        m2 = m1 + squares[1]
        m4 = m2 + squares[2] + squares[3]
        eq_ref[...] = parts[0] * lax.rsqrt(m1 + EPS)
        for ref, m, count in ((eh_ref, m2, 2), (ef_ref, m4, 4)):
            inv = lax.rsqrt(m + EPS)
            for c in range(count):
                ref[:, c * C : (c + 1) * C] = parts[c] * inv

    @pl.when(keeps)
    def _():
        near = ctx - z < SLOTS
        blk32[...] = jnp.zeros_like(blk32)

        @pl.when(near)
        def _():
            blk32[...] = zs[rows_of(((ctx - z) // NX) * 16 % 48, 16), :].astype(F32)

        @pl.loop(first_z, last_z + 1)
        def _(zz):
            @pl.when(zz != z)
            def _():
                pz_wait(zz).wait_recv()
                blk32[...] += rz[zz].astype(F32)
        embed(blk32[...])

    @pl.when(sends_b)
    def _():
        pb_copy(ctx).wait_recv()
        embed(rb[...].astype(F32))

    @pl.when(ctx == LAST)
    def _():
        embed(s2b[(HALF - 1) * 16 : HALF * 16, :].astype(F32))

    total = total_of(gx, NX * nc, x_pairs)
    qgain_ref[...] = total[0:1]
    kgain_ref[...] = total[1:2]

    @pl.loop(0, G)
    def _(g):
        for i in range(4):
            halo_copy(g, i).wait_send()
            grad_copy(g, i).wait_send()
    row_copy(0).wait_send()
    row_copy(1).wait_send()

    def sent(w):
        for i in range(1, NX):
            cx_copy(w, i).wait_send()

        @pl.when(z + w != ctx)
        def _():
            pz_copy(w).wait_send()

    each_slot(sent)
    other_slots(lambda w: px_copy(w).wait_send())

    @pl.when(keeps)
    def _():
        each_z(lambda zz: cz_copy(zz).wait_send())

    @pl.when(sends_b)
    def _():
        cb_copy(ctx).wait_send()

    @pl.when(ctx == LAST)
    def _():
        @pl.loop(HALF, LAST)
        def _(c):
            pb_copy(c).wait_send()
    for pair in z_pairs + y_pairs + x_pairs:
        pair[0].wait_send()


def emit(*refs):
    srcs, dsts, held, sem = refs[:8], refs[8:16], refs[16:24], refs[24]
    moves = []
    for i in range(8):
        parts = 4 if i == 3 else 1
        size = srcs[i].shape[0] // parts
        for p in range(parts):
            at = pl.ds(p * size, size)
            n = len(moves)
            first = pltpu.make_async_copy(srcs[i].at[at], held[i].at[at], sem.at[0, n])
            moves.append((first, pltpu.make_async_copy(held[i].at[at], dsts[i].at[at], sem.at[1, n])))
    order = sorted(range(len(moves)), key=lambda n: not 3 <= n < 7)
    for n in order:
        moves[n][0].start()
    for n in order:
        moves[n][0].wait()
        moves[n][1].start()
    for n in order:
        moves[n][1].wait()


def body(queries, keys, values, doc_lengths, cotangent, query_gain, key_gain):
    nc = 2 if lax.axis_size("dp") > 1 else 1
    ny = lax.axis_size("dp") // nc
    vmem, dma = pltpu.VMEM, pltpu.SemaphoreType.DMA
    scratch = [
        vmem((T, W), BF16),
        vmem((T, G * T), BF16),
        vmem((T, G * T), BF16),
        vmem((G, 4, T, T), BF16),
        vmem((G, 3 * T, T), BF16),
        vmem((G, 3 * T, T), F32),
        vmem((G, T, 1), F32),
        vmem((G, 3 * T, T), BF16),
        vmem((G, R * T, T), BF16),
        vmem((G, R * T, T), F32),
        vmem((G, R * T, 1), F32),
        vmem((G, R * T, 3 * T), F32),
        vmem((T, 3 * T), F32),
        vmem((T, W), BF16),
        vmem((T, W), F32),
        vmem((T, W), F32),
        vmem((T, W), BF16),
        vmem((2, 1, W), F32),
        vmem((2, 1, W), F32),
        vmem((16, C), F32),
        vmem((32, C), BF16),
        vmem((SLOTS * 32, C), BF16),
        vmem((HALF * 32, C), BF16),
        vmem((SLOTS * 16, C), BF16),
        vmem((HALF * 16, C), BF16),
        vmem((NX, 48, C), BF16),
        vmem((48, C), BF16),
        vmem((NZ, 16, C), BF16),
        vmem((16, C), BF16),
        vmem((R * T, 3 * T), BF16),
        vmem((G, R * T, 3 * T), BF16),
        vmem((R * T, T), BF16),
        vmem((G, R * T, T), F32),
        vmem((G, 4, T, T), BF16),
        vmem((G, 4, T, T), BF16),
        vmem((G, T, T), F32),
        vmem((G, T, T), F32),
        vmem((NZ, 8, T), F32),
        vmem((ny, 8, T), F32),
        vmem((nc * NX, 8, T), F32),
        dma((3,)),
        dma((G, 4)), dma((G, 4)),
        dma((2,)), dma((2,)),
        dma((NZ,)), dma((SLOTS,)),
        dma((SLOTS, NX)), dma((SLOTS,)),
        dma((1,)), dma((HALF,)),
        dma((SLOTS,)), dma((NX, 3)),
        dma((3,)), dma((NZ,)),
        dma((HALF,)), dma((1,)),
        dma((G, 4)), dma((G, 4)),
        dma((NZ,)), dma((NZ,)),
        dma((ny,)), dma((ny,)),
        dma((nc * NX,)), dma((nc * NX,)),
    ]
    shape = jax.ShapeDtypeStruct
    outs = pl.pallas_call(
        functools.partial(kernel, ny, nc),
        out_shape=(
            shape((4, C), F32),
            shape((4, 2 * C), F32),
            shape((4, W), F32),
            shape((T, W), BF16),
            shape((T, G * T), BF16),
            shape((T, G * T), BF16),
            shape((1, T), F32),
            shape((1, T), F32),
        ),
        in_specs=[pl.BlockSpec(memory_space=pl.ANY)] * 3 + [pl.BlockSpec(memory_space=pltpu.VMEM)] * 4,
        out_specs=tuple([pl.BlockSpec(memory_space=pltpu.VMEM)] * 8),
        scratch_shapes=scratch,
        compiler_params=pltpu.CompilerParams(
            collective_id=0, has_side_effects=True, vmem_limit_bytes=56 * 1024 * 1024
        ),
    )(
        queries[0], keys[0], values[0], doc_lengths, cotangent[0],
        query_gain.reshape(1, T), key_gain.reshape(1, T),
    )
    outs = pl.pallas_call(
        emit,
        out_shape=tuple(shape(out.shape, out.dtype) for out in outs),
        in_specs=[pl.BlockSpec(memory_space=pl.ANY)] * 8,
        out_specs=tuple([pl.BlockSpec(memory_space=pl.ANY)] * 8),
        scratch_shapes=[vmem(out.shape, out.dtype) for out in outs] + [dma((2, 11))],
    )(*outs)
    eq, eh, ef, gq, gk, gv, qgain, kgain = outs
    return (eq[None], eh[None], ef[None], gq[None], gk[None], gv[None], qgain[0], kgain[0])


def solution(mesh):
    rows = P("dp", "ctx", None)
    in_specs = (rows, rows, rows, P("dp", None), rows, P(), P())
    out_specs = (rows, rows, rows, rows, rows, rows, P(), P())
    return jax.shard_map(body, mesh=mesh, in_specs=in_specs, out_specs=out_specs, check_vma=False)
```

```python
import functools
import math

import jax
import jax.numpy as jnp
from jax import lax
from jax.experimental import pallas as pl
from jax.experimental.pallas import tpu as pltpu
from jax.sharding import PartitionSpec as P

EPS = 1e-06
T = 128
G = 8
R = 4
W = 4096
NX, NZ = 4, 8
C = 1024
SCALE = 1.0 / math.sqrt(T)
LOG2E = 1.4426950408889634
NEG = -1e30
F32, BF16 = jnp.float32, jnp.bfloat16
MESH = pl.DeviceIdType.MESH
LAST = NX * NZ - 1
HALF = NX * NZ // 2
SLOTS = 9
NT = (((1,), (1,)), ((), ()))
TN = (((0,), (0,)), ((), ()))


def iota(shape, dim):
    return lax.broadcasted_iota(jnp.int32, shape, dim)


def dot(a, b, dims=(((1,), (0,)), ((), ()))):
    return lax.dot_general(a, b, dims, preferred_element_type=F32)


def rows_of(start, size):
    return pl.ds(pl.multiple_of(start, 16), size)


def cols_of(start, size):
    return pl.ds(pl.multiple_of(start, 128), size)


def kernel(
    ny, nc,
    q_ref, k_ref, v_ref, len_ref, cot_ref, qg_ref, kg_ref,
    eq_ref, eh_ref, ef_ref, gq_ref, gk_ref, gv_ref, qgain_ref, kgain_ref,
    qv, kv, vv, halo, kn, uk, ik, vw, qn, uq, iq, pr, bias, pool, tokc, ga, rows_s, rows_r,
    blk32, blk, cot_a, cot_b, s2, s2b, rx, zs, rz, rb, dss, lows, dos, dqs, dh_s, dh_r, dk_own, dv_own,
    gz, gy, gx,
    l_sem, h_snd, h_rcv, r_snd, r_rcv, cz_snd, cz_rcv, cx_snd, cx_rcv, cf_snd, cf_rcv, cb_snd, cb_rcv,
    px_snd, px_rcv, pz_snd, pz_rcv, pb_snd, pb_rcv, d_snd, d_rcv,
    gz_snd, gz_rcv, gy_snd, gy_rcv, gx_snd, gx_rcv,
):
    dp, ctx = lax.axis_index("dp"), lax.axis_index("ctx")
    z, x = ctx // NX, ctx % NX
    y, core = dp // nc, dp % nc
    nxt, prv = (ctx + 1) % (NX * NZ), (ctx + NX * NZ - 1) % (NX * NZ)
    keeps = ctx < HALF
    sends_b = jnp.logical_and(ctx >= HALF, ctx < LAST)

    def at_z(i):
        return (dp, ((z + i) % NZ) * NX + x)

    def at_x(i):
        return (dp, z * NX + (x + i) % NX)

    def at_y(i):
        return (((y + i) % ny) * nc + core, ctx)

    loads = [
        pltpu.make_async_copy(src, dst, l_sem.at[i])
        for i, (src, dst) in enumerate(((k_ref, kv), (v_ref, vv), (q_ref, qv)))
    ]
    for load in loads:
        load.start()

    barrier = pltpu.get_barrier_semaphore()

    def greet(device):
        pl.semaphore_signal(barrier, inc=1, device_id=device, device_id_type=MESH)

    for i in range(1, NZ):
        greet(at_z(i))
    for i in range(1, NX):
        greet(at_x(i))
    for i in range(1, ny):
        greet(at_y(i))
    for j in range(1, nc):
        for i in range(NX):
            greet((y * nc + (core + j) % nc, z * NX + (x + i) % NX))

    @pl.when(x == NX - 1)
    def _():
        greet((dp, nxt))

    @pl.when(x == 0)
    def _():
        greet((dp, prv))

    @pl.when(sends_b)
    def _():
        greet((dp, LAST))

    @pl.when(ctx == LAST)
    def _():
        @pl.loop(HALF, LAST)
        def _(c):
            greet((dp, c))

    count = (NZ - 1) + (NX - 1) + (ny - 1) + NX * (nc - 1)
    edge = jnp.where(jnp.logical_or(x == 0, x == NX - 1), 1, 0)
    far = jnp.where(ctx == LAST, LAST - HALF, jnp.where(sends_b, 1, 0))
    arrivals = count + edge + far

    lens = jnp.broadcast_to(len_ref[...].astype(F32), (T, T))
    ii, jj = iota((T, T), 0), iota((T, T), 1)
    base = (ctx * T).astype(F32)

    def pick(cond, value, axis):
        return jnp.sum(jnp.where(cond, value, 0.0), axis=axis, keepdims=True)

    lens_col = pick(ii == jj, lens, 1)
    ends_col = pick(jj <= ii, lens, 1)
    ends_row = pick(ii <= jj, jnp.broadcast_to(lens_col, (T, T)), 0)
    starts = ends_row - lens[:1]
    ids_col = pick(base + ii.astype(F32) >= ends_row, 1.0, 1)
    key_pos = base - T + iota((T, 3 * T), 1).astype(F32)
    ids_row = jnp.where(key_pos[:1] < 0.0, -1.0, pick(key_pos >= ends_col, 1.0, 0))
    bias[...] = jnp.where(ids_col == ids_row, 0.0, NEG)
    own_row = ids_row[:, T : 2 * T]
    same = jnp.where(ids_col == own_row, 1.0, 0.0).astype(BF16)
    inv_len = 1.0 / pick(ids_col == jj.astype(F32), lens, 1)
    with_prv = jnp.where(ids_col == jnp.max(ids_row[:, :T], axis=1, keepdims=True), 1.0, 0.0)
    with_nxt = jnp.where(ids_col == jnp.min(ids_row[:, 2 * T :], axis=1, keepdims=True), 1.0, 0.0)

    for c in range(4):
        blk32[c * 4 : c * 4 + 4, :] = cot_ref[:, c * C : (c + 1) * C]
    high = blk32[...].astype(BF16)
    blk[:16, :] = high
    blk[16:, :] = (blk32[...] - high.astype(F32)).astype(BF16)

    pl.semaphore_wait(barrier, arrivals)

    def remote(src, dst, snd, rcv, device):
        return pltpu.make_async_remote_copy(
            src_ref=src, dst_ref=dst, send_sem=snd, recv_sem=rcv, device_id=device, device_id_type=MESH
        )

    def halo_copy(g, i):
        src = (kv if i < 2 else vv).at[:, cols_of(g * T, T)]
        return remote(src, halo.at[g, i], h_snd.at[g, i], h_rcv.at[g, i], (dp, nxt if i % 2 == 0 else prv))

    loads[0].wait()
    loads[1].wait()

    @pl.loop(0, G)
    def _(g):
        for i in range(4):
            halo_copy(g, i).start()

    def cz_copy(zz):
        return remote(blk, cot_a.at[rows_of((ctx - zz) * 32, 32)], cz_snd.at[zz], cz_rcv.at[ctx - zz], (dp, zz * NX + x))

    def cz_wait(w):
        return remote(blk, cot_a.at[rows_of(w * 32, 32)], cz_snd.at[0], cz_rcv.at[w], at_z(1))

    def cx_copy(w, i):
        own = cot_a.at[rows_of(w * 32, 32)]
        return remote(own, own, cx_snd.at[w, i], cx_rcv.at[w], at_x(i))

    def cf_copy(w, h):
        part = cot_a.at[rows_of(w * 32 + 16 * h, 16)]
        return remote(part, part, cf_snd.at[w], cf_rcv.at[w, h], at_x(1 if h == 0 else NX - 1))

    def by_column(i, fn):
        @pl.loop(0, SLOTS)
        def _(w):
            @pl.when((z + w) % NX == (x + i) % NX)
            def _():
                fn(w)

    def cb_copy(c):
        return remote(blk, cot_b.at[rows_of((c - HALF) * 32, 32)], cb_snd.at[0], cb_rcv.at[c - HALF], (dp, LAST))

    first_z, last_z = jnp.maximum(ctx - (SLOTS - 1), 0), jnp.minimum(ctx, NZ - 1)
    first_w = (x + NX * NZ - z) % NX

    def each_slot(fn):
        @pl.loop(0, 3)
        def _(j):
            w = first_w + NX * j

            @pl.when(w < SLOTS)
            def _():
                fn(w)

    def each_z(fn):
        @pl.loop(first_z, last_z + 1)
        def _(zz):
            @pl.when(zz != z)
            def _():
                fn(zz)

    @pl.when(keeps)
    def _():
        @pl.when(ctx - z < SLOTS)
        def _():
            cot_a[rows_of((ctx - z) * 32, 32), :] = blk[...]
        each_z(lambda zz: cz_copy(zz).start())

    @pl.when(sends_b)
    def _():
        cb_copy(ctx).start()

    @pl.when(ctx == LAST)
    def _():
        cot_b[(HALF - 1) * 32 : HALF * 32, :] = blk[...]

    q_gain, k_gain = qg_ref[...], kg_ref[...]

    loads[2].wait()

    @pl.loop(0, G)
    def _(g):
        for p in range(R):
            rows = slice(p * T, (p + 1) * T)
            raw = qv[:, cols_of(g * (R * T) + p * T, T)].astype(F32)
            inv = lax.rsqrt(jnp.mean(raw * raw, axis=-1, keepdims=True) + EPS)
            unit = raw * inv
            uq[g, rows, :] = unit
            iq[g, rows, :] = inv
            qn[g, rows, :] = (unit * q_gain).astype(BF16)

    def forward(g):
        for i in range(4):
            halo_copy(g, i).wait_recv()
        cols = cols_of(g * T, T)
        for i, raw in enumerate((halo[g, 0], kv[:, cols], halo[g, 1])):
            raw = raw.astype(F32)
            inv = lax.rsqrt(jnp.mean(raw * raw, axis=-1, keepdims=True) + EPS)
            unit = raw * inv
            uk[g, i * T : (i + 1) * T, :] = unit
            kn[g, i * T : (i + 1) * T, :] = (unit * k_gain).astype(BF16)
            if i == 1:
                ik[g] = inv
        vw[g, :T, :] = halo[g, 2]
        vw[g, T : 2 * T, :] = vv[:, cols]
        vw[g, 2 * T :, :] = halo[g, 3]
        products = dot(qn[g], kn[g], NT)
        for p in range(R):
            rows = slice(p * T, (p + 1) * T)
            s = products[rows] * (SCALE * LOG2E) + bias[...]
            powers = jnp.exp2(s - jnp.max(s, axis=-1, keepdims=True))
            probs = powers * (1.0 / jnp.sum(powers, axis=-1, keepdims=True))
            pr[g, rows, :] = probs
            lows[g, rows, :] = probs.astype(BF16)
        mixed = dot(lows[g], vw[g]).astype(BF16)
        for p in range(R):
            cols = cols_of(g * (R * T) + p * T, T)
            sums = dot(same, mixed[p * T : (p + 1) * T])
            pool[:, cols] = sums
            rows_s[0, :, cols] = sums[:1]
            rows_s[1, :, cols] = sums[T - 1 :]

    @pl.loop(0, G // 2)
    def _(g):
        forward(g)

    def along_x(w):
        @pl.when(z + w != z * NX + x)
        def _():
            cz_wait(w).wait_recv()
        for i in (1, NX - 1):
            cx_copy(w, i).start()

    each_slot(along_x)

    @pl.loop(G // 2, G)
    def _(g):
        forward(g)

    def row_copy(i):
        return remote(rows_s.at[i], rows_r.at[1 - i], r_snd.at[i], r_rcv.at[1 - i], (dp, prv if i == 0 else nxt))

    row_copy(0).start()
    row_copy(1).start()
    def pass_on(w, h):
        cx_copy(w, 1).wait_recv()
        cf_copy(w, h).start()

    by_column(NX - 1, lambda w: pass_on(w, 0))
    by_column(1, lambda w: pass_on(w, 1))

    def passed(w):
        for h in range(2):
            cf_copy(w, h).wait_recv()

    by_column(2, passed)

    def docs_of(count):
        rr = iota((1, count), 1)
        return ((rr >> 5) * 4 + (rr & 3)).astype(F32), (rr >> 2) & 3

    doc_a, quarter_a = docs_of(SLOTS * 32)
    doc_a = doc_a + (z * 4).astype(F32)
    doc_b, quarter_b = docs_of(HALF * 32)
    doc_b = doc_b + 4.0 * HALF
    def spread(doc, quarter, blocks, add):
        hits = ids_col == doc
        hot = jnp.concatenate(
            [jnp.where(jnp.logical_and(hits, quarter == c), 1.0, 0.0).astype(BF16) for c in range(4)], axis=0
        )
        for h in range(4):
            term = dot(hot, blocks[:, h * 256 : (h + 1) * 256])
            for c in range(4):
                cols = slice(c * C + h * 256, c * C + (h + 1) * 256)
                rows = term[c * T : (c + 1) * T]
                tokc[:, cols] = tokc[:, cols] + rows if add else rows

    spread(doc_a, quarter_a, cot_a, False)

    @pl.when(ctx == LAST)
    def _():
        @pl.loop(HALF, LAST)
        def _(c):
            cb_copy(c).wait_recv()
        spread(doc_b, quarter_b, cot_b, True)

    row_copy(0).wait_recv()
    row_copy(1).wait_recv()
    norms, inners = [], []
    for c in range(8):
        cols = slice(c * 512, (c + 1) * 512)
        p = (pool[:, cols] + with_prv * rows_r[0, :, cols] + with_nxt * rows_r[1, :, cols]) * inv_len
        pool[:, cols] = p
        norms.append(jnp.sum(p * p, axis=1, keepdims=True))
        inners.append(jnp.sum(p * tokc[:, cols], axis=1, keepdims=True))

    def gathered(count, first):
        rc, tc = iota((count * 16, T), 0), iota((count * 16, T), 1)
        doc_of = first + (rc >> 4) * 4 + (rc & 3)
        here = pick(doc_of == tc, starts, 1) - base == tc.astype(F32)
        part = (rc >> 2) & 3
        hots = [jnp.where(jnp.logical_and(here, part == c), 1.0, 0.0).astype(BF16) for c in range(4)]
        halves = []
        for h in range(2):
            total = None
            for c in range(4):
                term = dot(hots[c], pool[:, c * C + h * 512 : c * C + (h + 1) * 512].astype(BF16))
                total = term if total is None else total + term
            halves.append(total.astype(BF16))
        return halves

    halves = gathered(SLOTS, z * 4)
    for h in range(2):
        s2[:, h * 512 : (h + 1) * 512] = halves[h]

    def px_copy(w):
        dst = rx.at[x, rows_of((w // NX) * 16, 16)]
        return remote(s2.at[rows_of(w * 16, 16)], dst, px_snd.at[w], px_rcv.at[x, w // NX], (dp, z * NX + (z + w) % NX))

    def px_wait(w, xx):
        dst = rx.at[xx, rows_of((w // NX) * 16, 16)]
        return remote(s2.at[rows_of(0, 16)], dst, px_snd.at[0], px_rcv.at[xx, w // NX], at_x(1))

    def other_slots(fn):
        @pl.loop(0, SLOTS)
        def _(w):
            @pl.when((z + w) % NX != x)
            def _():
                fn(w)

    other_slots(lambda w: px_copy(w).start())

    def pb_copy(c):
        return remote(s2b.at[rows_of((c - HALF) * 16, 16)], rb, pb_snd.at[c - HALF], pb_rcv.at[0], (dp, c))

    @pl.when(ctx == LAST)
    def _():
        halves = gathered(HALF, 4 * HALF)
        for h in range(2):
            s2b[:, h * 512 : (h + 1) * 512] = halves[h]

        @pl.loop(HALF, LAST)
        def _(c):
            pb_copy(c).start()

    by_quarter = [norms[2 * c] + norms[2 * c + 1] for c in range(4)]
    inner_quarter = [inners[2 * c] + inners[2 * c + 1] for c in range(4)]
    n1 = by_quarter[0]
    n2 = n1 + by_quarter[1]
    n4 = n2 + by_quarter[2] + by_quarter[3]
    d1 = inner_quarter[0]
    d2 = d1 + inner_quarter[1]
    d4 = d2 + inner_quarter[2] + inner_quarter[3]
    i1, i2, i4 = lax.rsqrt(n1 + EPS), lax.rsqrt(n2 + EPS), lax.rsqrt(n4 + EPS)
    b1, b2, b4 = i1 * i1 * i1 * d1, i2 * i2 * i2 * d2, i4 * i4 * i4 * d4
    left = [i1 + i2 + i4, i2 + i4, i4, i4]
    right = [b1 + b2 + b4, b2 + b4, b4, b4]
    for c in range(8):
        cols = slice(c * 512, (c + 1) * 512)
        ga[:, cols] = ((left[c // 2] * tokc[:, cols] - right[c // 2] * pool[:, cols]) * inv_len).astype(BF16)

    def grad_copy(g, i):
        return remote(
            dh_s.at[g, i], dh_r.at[g, i], d_snd.at[g, i], d_rcv.at[g, i], (dp, prv if i % 2 == 0 else nxt)
        )

    def scores(g, carry):
        q_sum, k_sum = carry
        for p in range(R):
            dos[p * T : (p + 1) * T, :] = ga[:, cols_of(g * (R * T) + p * T, T)]
        products = dot(dos[...], vw[g], NT)
        for p in range(R):
            rows = slice(p * T, (p + 1) * T)
            probs, dprobs = pr[g, rows, :], products[rows]
            inner = jnp.sum(probs * dprobs, axis=-1, keepdims=True)
            dss[rows, :] = (probs * (dprobs - inner)).astype(BF16)
        dq = dot(dss[...], kn[g]) * SCALE
        dqs[g] = dq
        q_sum = q_sum + jnp.sum(dq * uq[g], axis=0, keepdims=True)
        dk = dot(dss[...], qn[g], TN) * SCALE
        k_sum = k_sum + jnp.sum(dk * uk[g], axis=0, keepdims=True)
        dh_s[g, 0] = dk[:T].astype(BF16)
        dh_s[g, 1] = dk[2 * T :].astype(BF16)
        for i in range(2):
            grad_copy(g, i).start()
        dk_own[g] = dk[T : 2 * T]
        return q_sum, k_sum

    def finish(g):
        for p in range(R):
            cols = cols_of(g * (R * T) + p * T, T)
            rows = slice(p * T, (p + 1) * T)
            dos[rows, :] = ga[:, cols]
            unit = uq[g, rows, :]
            scaled = dqs[g, rows, :] * q_gain
            mean = jnp.mean(scaled * unit, axis=-1, keepdims=True)
            gq_ref[:, cols] = (iq[g, rows, :] * (scaled - unit * mean)).astype(BF16)
        dv = dot(lows[g], dos[...], TN)
        dh_s[g, 2] = dv[:T].astype(BF16)
        dh_s[g, 3] = dv[2 * T :].astype(BF16)
        for i in range(2, 4):
            grad_copy(g, i).start()
        dv_own[g] = dv[T : 2 * T]

    zero = jnp.zeros((1, T), F32)
    q_sum, k_sum = lax.fori_loop(0, G, scores, (zero, zero))

    def total_of(slots, count, copies):
        for copy in copies:
            copy[1].wait_recv()
        total = slots[0]
        for i in range(1, count):
            total = total + slots[i]
        return total

    def send(copies):
        for copy in copies:
            copy[0].start()

    def gain_pair(slots, snd, rcv, i, place, other, device):
        return (
            remote(slots.at[place], slots.at[place], snd.at[i], rcv.at[place], device),
            remote(slots.at[other], slots.at[other], snd.at[i], rcv.at[other], device),
        )

    r8 = iota((8, T), 0)
    gz[z] = jnp.where(r8 == 0, q_sum, jnp.where(r8 == 1, k_sum, 0.0))
    z_pairs = [gain_pair(gz, gz_snd, gz_rcv, i, z, (z + i) % NZ, at_z(i)) for i in range(1, NZ)]
    y_pairs = [gain_pair(gy, gy_snd, gy_rcv, i, y, (y + i) % ny, at_y(i)) for i in range(1, ny)]
    spot = core * NX + x
    x_pairs = []
    for j in range(nc):
        for i in range(NX):
            if i or j:
                there = (core + j) % nc
                other = there * NX + (x + i) % NX
                device = (y * nc + there, z * NX + (x + i) % NX)
                x_pairs.append(gain_pair(gx, gx_snd, gx_rcv, j * NX + i, spot, other, device))
    send(z_pairs)

    def pz_copy(w):
        src = zs.at[rows_of((w // NX) * 16, 16)]
        return remote(src, rz.at[z], pz_snd.at[w // NX], pz_rcv.at[z], (dp, z + w))

    def pz_wait(zz):
        return remote(zs.at[rows_of(0, 16)], rz.at[zz], pz_snd.at[0], pz_rcv.at[zz], at_z(1))

    def merge(w):
        rows = s2[rows_of(w * 16, 16), :].astype(F32)
        for i in range(1, NX):
            xx = (x + i) % NX
            px_wait(w, xx).wait_recv()
            rows = rows + rx[xx, rows_of((w // NX) * 16, 16), :].astype(F32)
        zs[rows_of((w // NX) * 16, 16), :] = rows.astype(BF16)

        @pl.when(z + w != ctx)
        def _():
            pz_copy(w).start()

    @pl.loop(0, G // 2)
    def _(g):
        finish(g)

    gy[y] = total_of(gz, NZ, z_pairs)
    send(y_pairs)

    @pl.loop(G // 2, G)
    def _(g):
        finish(g)

    each_slot(merge)

    gx[spot] = total_of(gy, ny, y_pairs)
    send(x_pairs)

    @pl.loop(0, G)
    def _(g):
        for i in range(4):
            grad_copy(g, i).wait_recv()
        cols = cols_of(g * T, T)
        dk = dk_own[g] + (dh_r[g, 0].astype(F32) + dh_r[g, 1].astype(F32))
        dv = dv_own[g] + (dh_r[g, 2].astype(F32) + dh_r[g, 3].astype(F32))
        unit = uk[g, T : 2 * T, :]
        scaled = dk * k_gain
        mean = jnp.mean(scaled * unit, axis=-1, keepdims=True)
        gk_ref[:, cols] = (ik[g] * (scaled - unit * mean)).astype(BF16)
        gv_ref[:, cols] = dv.astype(BF16)

    def embed(rows):
        parts = [rows[c * 4 : c * 4 + 4] for c in range(4)]
        squares = [jnp.sum(part * part, axis=1, keepdims=True) for part in parts]
        m1 = squares[0]
        m2 = m1 + squares[1]
        m4 = m2 + squares[2] + squares[3]
        eq_ref[...] = parts[0] * lax.rsqrt(m1 + EPS)
        for ref, m, count in ((eh_ref, m2, 2), (ef_ref, m4, 4)):
            inv = lax.rsqrt(m + EPS)
            for c in range(count):
                ref[:, c * C : (c + 1) * C] = parts[c] * inv

    @pl.when(keeps)
    def _():
        near = ctx - z < SLOTS
        blk32[...] = jnp.zeros_like(blk32)

        @pl.when(near)
        def _():
            blk32[...] = zs[rows_of(((ctx - z) // NX) * 16 % 48, 16), :].astype(F32)

        @pl.loop(first_z, last_z + 1)
        def _(zz):
            @pl.when(zz != z)
            def _():
                pz_wait(zz).wait_recv()
                blk32[...] += rz[zz].astype(F32)
        embed(blk32[...])

    @pl.when(sends_b)
    def _():
        pb_copy(ctx).wait_recv()
        embed(rb[...].astype(F32))

    @pl.when(ctx == LAST)
    def _():
        embed(s2b[(HALF - 1) * 16 : HALF * 16, :].astype(F32))

    total = total_of(gx, NX * nc, x_pairs)
    qgain_ref[...] = total[0:1]
    kgain_ref[...] = total[1:2]

    @pl.loop(0, G)
    def _(g):
        for i in range(4):
            halo_copy(g, i).wait_send()
            grad_copy(g, i).wait_send()
    row_copy(0).wait_send()
    row_copy(1).wait_send()

    def sent(w):
        for i in (1, NX - 1):
            cx_copy(w, i).wait_send()

        @pl.when(z + w != ctx)
        def _():
            pz_copy(w).wait_send()

    each_slot(sent)
    by_column(NX - 1, lambda w: cf_copy(w, 0).wait_send())
    by_column(1, lambda w: cf_copy(w, 1).wait_send())
    other_slots(lambda w: px_copy(w).wait_send())

    @pl.when(keeps)
    def _():
        each_z(lambda zz: cz_copy(zz).wait_send())

    @pl.when(sends_b)
    def _():
        cb_copy(ctx).wait_send()

    @pl.when(ctx == LAST)
    def _():
        @pl.loop(HALF, LAST)
        def _(c):
            pb_copy(c).wait_send()
    for pair in z_pairs + y_pairs + x_pairs:
        pair[0].wait_send()


def emit(*refs):
    srcs, dsts, held, sem = refs[:8], refs[8:16], refs[16:24], refs[24]
    moves = []
    for i in range(8):
        parts = 4 if i == 3 else 1
        size = srcs[i].shape[0] // parts
        for p in range(parts):
            at = pl.ds(p * size, size)
            n = len(moves)
            first = pltpu.make_async_copy(srcs[i].at[at], held[i].at[at], sem.at[0, n])
            moves.append((first, pltpu.make_async_copy(held[i].at[at], dsts[i].at[at], sem.at[1, n])))
    order = sorted(range(len(moves)), key=lambda n: not 3 <= n < 7)
    for n in order:
        moves[n][0].start()
    for n in order:
        moves[n][0].wait()
        moves[n][1].start()
    for n in order:
        moves[n][1].wait()


def body(queries, keys, values, doc_lengths, cotangent, query_gain, key_gain):
    nc = 2 if lax.axis_size("dp") > 1 else 1
    ny = lax.axis_size("dp") // nc
    vmem, dma = pltpu.VMEM, pltpu.SemaphoreType.DMA
    scratch = [
        vmem((T, W), BF16),
        vmem((T, G * T), BF16),
        vmem((T, G * T), BF16),
        vmem((G, 4, T, T), BF16),
        vmem((G, 3 * T, T), BF16),
        vmem((G, 3 * T, T), F32),
        vmem((G, T, 1), F32),
        vmem((G, 3 * T, T), BF16),
        vmem((G, R * T, T), BF16),
        vmem((G, R * T, T), F32),
        vmem((G, R * T, 1), F32),
        vmem((G, R * T, 3 * T), F32),
        vmem((T, 3 * T), F32),
        vmem((T, W), F32),
        vmem((T, W), F32),
        vmem((T, W), BF16),
        vmem((2, 1, W), F32),
        vmem((2, 1, W), F32),
        vmem((16, C), F32),
        vmem((32, C), BF16),
        vmem((SLOTS * 32, C), BF16),
        vmem((HALF * 32, C), BF16),
        vmem((SLOTS * 16, C), BF16),
        vmem((HALF * 16, C), BF16),
        vmem((NX, 48, C), BF16),
        vmem((48, C), BF16),
        vmem((NZ, 16, C), BF16),
        vmem((16, C), BF16),
        vmem((R * T, 3 * T), BF16),
        vmem((G, R * T, 3 * T), BF16),
        vmem((R * T, T), BF16),
        vmem((G, R * T, T), F32),
        vmem((G, 4, T, T), BF16),
        vmem((G, 4, T, T), BF16),
        vmem((G, T, T), F32),
        vmem((G, T, T), F32),
        vmem((NZ, 8, T), F32),
        vmem((ny, 8, T), F32),
        vmem((nc * NX, 8, T), F32),
        dma((3,)),
        dma((G, 4)), dma((G, 4)),
        dma((2,)), dma((2,)),
        dma((NZ,)), dma((SLOTS,)),
        dma((SLOTS, NX)), dma((SLOTS,)),
        dma((SLOTS,)), dma((SLOTS, 2)),
        dma((1,)), dma((HALF,)),
        dma((SLOTS,)), dma((NX, 3)),
        dma((3,)), dma((NZ,)),
        dma((HALF,)), dma((1,)),
        dma((G, 4)), dma((G, 4)),
        dma((NZ,)), dma((NZ,)),
        dma((ny,)), dma((ny,)),
        dma((nc * NX,)), dma((nc * NX,)),
    ]
    shape = jax.ShapeDtypeStruct
    outs = pl.pallas_call(
        functools.partial(kernel, ny, nc),
        out_shape=(
            shape((4, C), F32),
            shape((4, 2 * C), F32),
            shape((4, W), F32),
            shape((T, W), BF16),
            shape((T, G * T), BF16),
            shape((T, G * T), BF16),
            shape((1, T), F32),
            shape((1, T), F32),
        ),
        in_specs=[pl.BlockSpec(memory_space=pl.ANY)] * 3 + [pl.BlockSpec(memory_space=pltpu.VMEM)] * 4,
        out_specs=tuple([pl.BlockSpec(memory_space=pltpu.VMEM)] * 8),
        scratch_shapes=scratch,
        compiler_params=pltpu.CompilerParams(
            collective_id=0, has_side_effects=True, vmem_limit_bytes=56 * 1024 * 1024
        ),
    )(
        queries[0], keys[0], values[0], doc_lengths, cotangent[0],
        query_gain.reshape(1, T), key_gain.reshape(1, T),
    )
    outs = pl.pallas_call(
        emit,
        out_shape=tuple(shape(out.shape, out.dtype) for out in outs),
        in_specs=[pl.BlockSpec(memory_space=pl.ANY)] * 8,
        out_specs=tuple([pl.BlockSpec(memory_space=pl.ANY)] * 8),
        scratch_shapes=[vmem(out.shape, out.dtype) for out in outs] + [dma((2, 11))],
    )(*outs)
    eq, eh, ef, gq, gk, gv, qgain, kgain = outs
    return (eq[None], eh[None], ef[None], gq[None], gk[None], gv[None], qgain[0], kgain[0])


def solution(mesh):
    rows = P("dp", "ctx", None)
    in_specs = (rows, rows, rows, P("dp", None), rows, P(), P())
    out_specs = (rows, rows, rows, rows, rows, rows, P(), P())
    return jax.shard_map(body, mesh=mesh, in_specs=in_specs, out_specs=out_specs, check_vma=False)
```

```python
import functools
import math

import jax
import jax.numpy as jnp
from jax import lax
from jax.experimental import pallas as pl
from jax.experimental.pallas import tpu as pltpu
from jax.sharding import PartitionSpec as P

EPS = 1e-06
T = 128
G = 8
R = 4
W = 4096
NX, NZ = 4, 8
C = 1024
SCALE = 1.0 / math.sqrt(T)
LOG2E = 1.4426950408889634
NEG = -1e30
F32, BF16 = jnp.float32, jnp.bfloat16
MESH = pl.DeviceIdType.MESH
LAST = NX * NZ - 1
HALF = NX * NZ // 2
SLOTS = 9
NT = (((1,), (1,)), ((), ()))
TN = (((0,), (0,)), ((), ()))


def iota(shape, dim):
    return lax.broadcasted_iota(jnp.int32, shape, dim)


def dot(a, b, dims=(((1,), (0,)), ((), ()))):
    return lax.dot_general(a, b, dims, preferred_element_type=F32)


def rows_of(start, size):
    return pl.ds(pl.multiple_of(start, 16), size)


def cols_of(start, size):
    return pl.ds(pl.multiple_of(start, 128), size)


def kernel(
    ny, nc,
    q_ref, k_ref, v_ref, len_ref, cot_ref, qg_ref, kg_ref,
    eq_ref, eh_ref, ef_ref, gq_ref, gk_ref, gv_ref, qgain_ref, kgain_ref,
    qv, kv, vv, halo, kn, uk, ik, vw, qn, uq, iq, pr, bias, pool, tokc, ga, rows_s, rows_r,
    blk32, blk, cot_a, cot_b, s2, s2b, rx, zs, rz, rb, dss, lows, dos, dqs, dh_s, dh_r, dk_own, dv_own,
    gz, gy, gx,
    l_sem, h_snd, h_rcv, r_snd, r_rcv, cz_snd, cz_rcv, cx_snd, cx_rcv, cf_snd, cf_rcv, cb_snd, cb_rcv,
    px_snd, px_rcv, pz_snd, pz_rcv, pb_snd, pb_rcv, d_snd, d_rcv,
    gz_snd, gz_rcv, gy_snd, gy_rcv, gx_snd, gx_rcv,
):
    dp, ctx = lax.axis_index("dp"), lax.axis_index("ctx")
    z, x = ctx // NX, ctx % NX
    y, core = dp // nc, dp % nc
    nxt, prv = (ctx + 1) % (NX * NZ), (ctx + NX * NZ - 1) % (NX * NZ)
    keeps = ctx < HALF
    sends_b = jnp.logical_and(ctx >= HALF, ctx < LAST)

    def at_z(i):
        return (dp, ((z + i) % NZ) * NX + x)

    def at_x(i):
        return (dp, z * NX + (x + i) % NX)

    def at_y(i):
        return (((y + i) % ny) * nc + core, ctx)

    loads = [
        pltpu.make_async_copy(src, dst, l_sem.at[i])
        for i, (src, dst) in enumerate(((k_ref, kv), (v_ref, vv), (q_ref, qv)))
    ]
    for load in loads:
        load.start()

    barrier = pltpu.get_barrier_semaphore()

    def greet(device):
        pl.semaphore_signal(barrier, inc=1, device_id=device, device_id_type=MESH)

    for i in range(1, NZ):
        greet(at_z(i))
    for i in range(1, NX):
        greet(at_x(i))
    for i in range(1, ny):
        greet(at_y(i))
    for j in range(1, nc):
        for i in range(NX):
            greet((y * nc + (core + j) % nc, z * NX + (x + i) % NX))

    @pl.when(x == NX - 1)
    def _():
        greet((dp, nxt))

    @pl.when(x == 0)
    def _():
        greet((dp, prv))

    @pl.when(sends_b)
    def _():
        greet((dp, LAST))

    @pl.when(ctx == LAST)
    def _():
        @pl.loop(HALF, LAST)
        def _(c):
            greet((dp, c))

    count = (NZ - 1) + (NX - 1) + (ny - 1) + NX * (nc - 1)
    edge = jnp.where(jnp.logical_or(x == 0, x == NX - 1), 1, 0)
    far = jnp.where(ctx == LAST, LAST - HALF, jnp.where(sends_b, 1, 0))
    arrivals = count + edge + far

    lens = jnp.broadcast_to(len_ref[...].astype(F32), (T, T))
    ii, jj = iota((T, T), 0), iota((T, T), 1)
    base = (ctx * T).astype(F32)

    def pick(cond, value, axis):
        return jnp.sum(jnp.where(cond, value, 0.0), axis=axis, keepdims=True)

    lens_col = pick(ii == jj, lens, 1)
    ends_col = pick(jj <= ii, lens, 1)
    ends_row = pick(ii <= jj, jnp.broadcast_to(lens_col, (T, T)), 0)
    starts = ends_row - lens[:1]
    ids_col = pick(base + ii.astype(F32) >= ends_row, 1.0, 1)
    key_pos = base - T + iota((T, 3 * T), 1).astype(F32)
    ids_row = jnp.where(key_pos[:1] < 0.0, -1.0, pick(key_pos >= ends_col, 1.0, 0))
    bias[...] = jnp.where(ids_col == ids_row, 0.0, NEG)
    own_row = ids_row[:, T : 2 * T]
    same = jnp.where(ids_col == own_row, 1.0, 0.0).astype(BF16)
    inv_len = 1.0 / pick(ids_col == jj.astype(F32), lens, 1)
    with_prv = jnp.where(ids_col == jnp.max(ids_row[:, :T], axis=1, keepdims=True), 1.0, 0.0)
    with_nxt = jnp.where(ids_col == jnp.min(ids_row[:, 2 * T :], axis=1, keepdims=True), 1.0, 0.0)

    for c in range(4):
        blk32[c * 4 : c * 4 + 4, :] = cot_ref[:, c * C : (c + 1) * C]
    high = blk32[...].astype(BF16)
    blk[:16, :] = high
    blk[16:, :] = (blk32[...] - high.astype(F32)).astype(BF16)

    pl.semaphore_wait(barrier, arrivals)

    def remote(src, dst, snd, rcv, device):
        return pltpu.make_async_remote_copy(
            src_ref=src, dst_ref=dst, send_sem=snd, recv_sem=rcv, device_id=device, device_id_type=MESH
        )

    def halo_copy(g, i):
        src = (kv if i < 2 else vv).at[:, cols_of(g * T, T)]
        return remote(src, halo.at[g, i], h_snd.at[g, i], h_rcv.at[g, i], (dp, nxt if i % 2 == 0 else prv))

    loads[0].wait()
    loads[1].wait()

    @pl.loop(0, G)
    def _(g):
        for i in range(4):
            halo_copy(g, i).start()

    def cz_copy(zz):
        return remote(blk, cot_a.at[rows_of((ctx - zz) * 32, 32)], cz_snd.at[zz], cz_rcv.at[ctx - zz], (dp, zz * NX + x))

    def cz_wait(w):
        return remote(blk, cot_a.at[rows_of(w * 32, 32)], cz_snd.at[0], cz_rcv.at[w], at_z(1))

    def cx_copy(w, i):
        own = cot_a.at[rows_of(w * 32, 32)]
        return remote(own, own, cx_snd.at[w, i], cx_rcv.at[w], at_x(i))

    def cf_copy(w, h):
        part = cot_a.at[rows_of(w * 32 + 16 * h, 16)]
        return remote(part, part, cf_snd.at[w], cf_rcv.at[w, h], at_x(1 if h == 0 else NX - 1))

    def by_column(i, fn):
        @pl.loop(0, SLOTS)
        def _(w):
            @pl.when((z + w) % NX == (x + i) % NX)
            def _():
                fn(w)

    def cb_copy(c):
        return remote(blk, cot_b.at[rows_of((c - HALF) * 32, 32)], cb_snd.at[0], cb_rcv.at[c - HALF], (dp, LAST))

    first_z, last_z = jnp.maximum(ctx - (SLOTS - 1), 0), jnp.minimum(ctx, NZ - 1)
    first_w = (x + NX * NZ - z) % NX

    def each_slot(fn):
        @pl.loop(0, 3)
        def _(j):
            w = first_w + NX * j

            @pl.when(w < SLOTS)
            def _():
                fn(w)

    def each_z(fn):
        @pl.loop(first_z, last_z + 1)
        def _(zz):
            @pl.when(zz != z)
            def _():
                fn(zz)

    @pl.when(keeps)
    def _():
        @pl.when(ctx - z < SLOTS)
        def _():
            cot_a[rows_of((ctx - z) * 32, 32), :] = blk[...]
        each_z(lambda zz: cz_copy(zz).start())

    @pl.when(sends_b)
    def _():
        cb_copy(ctx).start()

    @pl.when(ctx == LAST)
    def _():
        cot_b[(HALF - 1) * 32 : HALF * 32, :] = blk[...]

    q_gain, k_gain = qg_ref[...], kg_ref[...]

    loads[2].wait()

    @pl.loop(0, G)
    def _(g):
        for p in range(R):
            rows = slice(p * T, (p + 1) * T)
            raw = qv[:, cols_of(g * (R * T) + p * T, T)].astype(F32)
            inv = lax.rsqrt(jnp.mean(raw * raw, axis=-1, keepdims=True) + EPS)
            unit = raw * inv
            uq[g, rows, :] = unit
            iq[g, rows, :] = inv
            qn[g, rows, :] = (unit * q_gain).astype(BF16)

    def forward(g):
        for i in range(4):
            halo_copy(g, i).wait_recv()
        cols = cols_of(g * T, T)
        for i, raw in enumerate((halo[g, 0], kv[:, cols], halo[g, 1])):
            raw = raw.astype(F32)
            inv = lax.rsqrt(jnp.mean(raw * raw, axis=-1, keepdims=True) + EPS)
            unit = raw * inv
            uk[g, i * T : (i + 1) * T, :] = unit
            kn[g, i * T : (i + 1) * T, :] = (unit * k_gain).astype(BF16)
            if i == 1:
                ik[g] = inv
        vw[g, :T, :] = halo[g, 2]
        vw[g, T : 2 * T, :] = vv[:, cols]
        vw[g, 2 * T :, :] = halo[g, 3]
        products = dot(qn[g], kn[g], NT)
        for p in range(R):
            rows = slice(p * T, (p + 1) * T)
            s = products[rows] * (SCALE * LOG2E) + bias[...]
            powers = jnp.exp2(s - jnp.max(s, axis=-1, keepdims=True))
            probs = powers * (1.0 / jnp.sum(powers, axis=-1, keepdims=True))
            pr[g, rows, :] = probs
            lows[g, rows, :] = probs.astype(BF16)
        mixed = dot(lows[g], vw[g]).astype(BF16)
        for p in range(R):
            cols = cols_of(g * (R * T) + p * T, T)
            sums = dot(same, mixed[p * T : (p + 1) * T])
            pool[:, cols] = sums
            rows_s[0, :, cols] = sums[:1]
            rows_s[1, :, cols] = sums[T - 1 :]

    @pl.loop(0, G // 2)
    def _(g):
        forward(g)

    def along_x(w):
        @pl.when(z + w != z * NX + x)
        def _():
            cz_wait(w).wait_recv()
        for i in (1, NX - 1):
            cx_copy(w, i).start()

    each_slot(along_x)

    @pl.loop(G // 2, G)
    def _(g):
        forward(g)

    def row_copy(i):
        return remote(rows_s.at[i], rows_r.at[1 - i], r_snd.at[i], r_rcv.at[1 - i], (dp, prv if i == 0 else nxt))

    row_copy(0).start()
    row_copy(1).start()
    def pass_on(w, h):
        cx_copy(w, 1).wait_recv()
        cf_copy(w, h).start()

    by_column(NX - 1, lambda w: pass_on(w, 0))
    by_column(1, lambda w: pass_on(w, 1))

    def passed(w):
        for h in range(2):
            cf_copy(w, h).wait_recv()

    by_column(2, passed)

    def docs_of(count):
        rr = iota((1, count), 1)
        return ((rr >> 5) * 4 + (rr & 3)).astype(F32), (rr >> 2) & 3

    doc_a, quarter_a = docs_of(SLOTS * 32)
    doc_a = doc_a + (z * 4).astype(F32)
    doc_b, quarter_b = docs_of(HALF * 32)
    doc_b = doc_b + 4.0 * HALF
    def spread(doc, quarter, blocks, add):
        hits = ids_col == doc
        hot = jnp.concatenate(
            [jnp.where(jnp.logical_and(hits, quarter == c), 1.0, 0.0).astype(BF16) for c in range(4)], axis=0
        )
        for h in range(4):
            term = dot(hot, blocks[:, h * 256 : (h + 1) * 256])
            for c in range(4):
                cols = slice(c * C + h * 256, c * C + (h + 1) * 256)
                rows = term[c * T : (c + 1) * T]
                tokc[:, cols] = tokc[:, cols] + rows if add else rows

    spread(doc_a, quarter_a, cot_a, False)

    @pl.when(ctx == LAST)
    def _():
        @pl.loop(HALF, LAST)
        def _(c):
            cb_copy(c).wait_recv()
        spread(doc_b, quarter_b, cot_b, True)

    row_copy(0).wait_recv()
    row_copy(1).wait_recv()
    norms, inners = [], []
    for c in range(8):
        cols = slice(c * 512, (c + 1) * 512)
        p = (pool[:, cols] + with_prv * rows_r[0, :, cols] + with_nxt * rows_r[1, :, cols]) * inv_len
        pool[:, cols] = p
        norms.append(jnp.sum(p * p, axis=1, keepdims=True))
        inners.append(jnp.sum(p * tokc[:, cols], axis=1, keepdims=True))

    def gathered(count, first):
        rc, tc = iota((count * 16, T), 0), iota((count * 16, T), 1)
        doc_of = first + (rc >> 4) * 4 + (rc & 3)
        here = pick(doc_of == tc, starts, 1) - base == tc.astype(F32)
        part = (rc >> 2) & 3
        hots = [jnp.where(jnp.logical_and(here, part == c), 1.0, 0.0).astype(BF16) for c in range(4)]
        halves = []
        for h in range(2):
            total = None
            for c in range(4):
                term = dot(hots[c], pool[:, c * C + h * 512 : c * C + (h + 1) * 512].astype(BF16))
                total = term if total is None else total + term
            halves.append(total.astype(BF16))
        return halves

    halves = gathered(SLOTS, z * 4)
    for h in range(2):
        s2[:, h * 512 : (h + 1) * 512] = halves[h]

    def px_copy(w):
        dst = rx.at[x, rows_of((w // NX) * 16, 16)]
        return remote(s2.at[rows_of(w * 16, 16)], dst, px_snd.at[w], px_rcv.at[x, w // NX], (dp, z * NX + (z + w) % NX))

    def px_wait(w, xx):
        dst = rx.at[xx, rows_of((w // NX) * 16, 16)]
        return remote(s2.at[rows_of(0, 16)], dst, px_snd.at[0], px_rcv.at[xx, w // NX], at_x(1))

    def other_slots(fn):
        @pl.loop(0, SLOTS)
        def _(w):
            @pl.when((z + w) % NX != x)
            def _():
                fn(w)

    other_slots(lambda w: px_copy(w).start())

    def pb_copy(c):
        return remote(s2b.at[rows_of((c - HALF) * 16, 16)], rb, pb_snd.at[c - HALF], pb_rcv.at[0], (dp, c))

    @pl.when(ctx == LAST)
    def _():
        halves = gathered(HALF, 4 * HALF)
        for h in range(2):
            s2b[:, h * 512 : (h + 1) * 512] = halves[h]

        @pl.loop(HALF, LAST)
        def _(c):
            pb_copy(c).start()

    by_quarter = [norms[2 * c] + norms[2 * c + 1] for c in range(4)]
    inner_quarter = [inners[2 * c] + inners[2 * c + 1] for c in range(4)]
    n1 = by_quarter[0]
    n2 = n1 + by_quarter[1]
    n4 = n2 + by_quarter[2] + by_quarter[3]
    d1 = inner_quarter[0]
    d2 = d1 + inner_quarter[1]
    d4 = d2 + inner_quarter[2] + inner_quarter[3]
    i1, i2, i4 = lax.rsqrt(n1 + EPS), lax.rsqrt(n2 + EPS), lax.rsqrt(n4 + EPS)
    b1, b2, b4 = i1 * i1 * i1 * d1, i2 * i2 * i2 * d2, i4 * i4 * i4 * d4
    left = [i1 + i2 + i4, i2 + i4, i4, i4]
    right = [b1 + b2 + b4, b2 + b4, b4, b4]
    for c in range(8):
        cols = slice(c * 512, (c + 1) * 512)
        ga[:, cols] = ((left[c // 2] * tokc[:, cols] - right[c // 2] * pool[:, cols]) * inv_len).astype(BF16)

    def grad_copy(g, i):
        return remote(
            dh_s.at[g, i], dh_r.at[g, i], d_snd.at[g, i], d_rcv.at[g, i], (dp, prv if i % 2 == 0 else nxt)
        )

    def scores(g, carry):
        q_sum, k_sum = carry
        for p in range(R):
            dos[p * T : (p + 1) * T, :] = ga[:, cols_of(g * (R * T) + p * T, T)]
        products = dot(dos[...], vw[g], NT)
        for p in range(R):
            rows = slice(p * T, (p + 1) * T)
            probs, dprobs = pr[g, rows, :], products[rows]
            inner = jnp.sum(probs * dprobs, axis=-1, keepdims=True)
            dss[rows, :] = (probs * (dprobs - inner)).astype(BF16)
        dq = dot(dss[...], kn[g]) * SCALE
        dqs[g] = dq
        q_sum = q_sum + jnp.sum(dq * uq[g], axis=0, keepdims=True)
        dk = dot(dss[...], qn[g], TN) * SCALE
        k_sum = k_sum + jnp.sum(dk * uk[g], axis=0, keepdims=True)
        dh_s[g, 0] = dk[:T].astype(BF16)
        dh_s[g, 1] = dk[2 * T :].astype(BF16)
        for i in range(2):
            grad_copy(g, i).start()
        dk_own[g] = dk[T : 2 * T]
        return q_sum, k_sum

    def finish(g):
        for p in range(R):
            cols = cols_of(g * (R * T) + p * T, T)
            rows = slice(p * T, (p + 1) * T)
            dos[rows, :] = ga[:, cols]
            unit = uq[g, rows, :]
            scaled = dqs[g, rows, :] * q_gain
            mean = jnp.mean(scaled * unit, axis=-1, keepdims=True)
            gq_ref[:, cols] = (iq[g, rows, :] * (scaled - unit * mean)).astype(BF16)
        dv = dot(lows[g], dos[...], TN)
        dh_s[g, 2] = dv[:T].astype(BF16)
        dh_s[g, 3] = dv[2 * T :].astype(BF16)
        for i in range(2, 4):
            grad_copy(g, i).start()
        dv_own[g] = dv[T : 2 * T]

    zero = jnp.zeros((1, T), F32)
    q_sum, k_sum = lax.fori_loop(0, G, scores, (zero, zero))

    def total_of(slots, count, copies):
        for copy in copies:
            copy[1].wait_recv()
        total = slots[0]
        for i in range(1, count):
            total = total + slots[i]
        return total

    def send(copies):
        for copy in copies:
            copy[0].start()

    def gain_pair(slots, snd, rcv, i, place, other, device):
        return (
            remote(slots.at[place], slots.at[place], snd.at[i], rcv.at[place], device),
            remote(slots.at[other], slots.at[other], snd.at[i], rcv.at[other], device),
        )

    r8 = iota((8, T), 0)
    gz[z] = jnp.where(r8 == 0, q_sum, jnp.where(r8 == 1, k_sum, 0.0))
    z_pairs = [gain_pair(gz, gz_snd, gz_rcv, i, z, (z + i) % NZ, at_z(i)) for i in range(1, NZ)]
    y_pairs = [gain_pair(gy, gy_snd, gy_rcv, i, y, (y + i) % ny, at_y(i)) for i in range(1, ny)]
    spot = core * NX + x
    x_pairs = []
    for j in range(nc):
        for i in range(NX):
            if i or j:
                there = (core + j) % nc
                other = there * NX + (x + i) % NX
                device = (y * nc + there, z * NX + (x + i) % NX)
                x_pairs.append(gain_pair(gx, gx_snd, gx_rcv, j * NX + i, spot, other, device))
    send(z_pairs)

    def pz_copy(w):
        src = zs.at[rows_of((w // NX) * 16, 16)]
        return remote(src, rz.at[z], pz_snd.at[w // NX], pz_rcv.at[z], (dp, z + w))

    def pz_wait(zz):
        return remote(zs.at[rows_of(0, 16)], rz.at[zz], pz_snd.at[0], pz_rcv.at[zz], at_z(1))

    def merge(w):
        rows = s2[rows_of(w * 16, 16), :].astype(F32)
        for i in range(1, NX):
            xx = (x + i) % NX
            px_wait(w, xx).wait_recv()
            rows = rows + rx[xx, rows_of((w // NX) * 16, 16), :].astype(F32)
        zs[rows_of((w // NX) * 16, 16), :] = rows.astype(BF16)

        @pl.when(z + w != ctx)
        def _():
            pz_copy(w).start()

    @pl.loop(0, G)
    def _(g):
        finish(g)

    gy[y] = total_of(gz, NZ, z_pairs)
    send(y_pairs)

    each_slot(merge)

    gx[spot] = total_of(gy, ny, y_pairs)
    send(x_pairs)

    @pl.loop(0, G)
    def _(g):
        for i in range(4):
            grad_copy(g, i).wait_recv()
        cols = cols_of(g * T, T)
        dk = dk_own[g] + (dh_r[g, 0].astype(F32) + dh_r[g, 1].astype(F32))
        dv = dv_own[g] + (dh_r[g, 2].astype(F32) + dh_r[g, 3].astype(F32))
        unit = uk[g, T : 2 * T, :]
        scaled = dk * k_gain
        mean = jnp.mean(scaled * unit, axis=-1, keepdims=True)
        gk_ref[:, cols] = (ik[g] * (scaled - unit * mean)).astype(BF16)
        gv_ref[:, cols] = dv.astype(BF16)

    def embed(rows):
        parts = [rows[c * 4 : c * 4 + 4] for c in range(4)]
        squares = [jnp.sum(part * part, axis=1, keepdims=True) for part in parts]
        m1 = squares[0]
        m2 = m1 + squares[1]
        m4 = m2 + squares[2] + squares[3]
        eq_ref[...] = parts[0] * lax.rsqrt(m1 + EPS)
        for ref, m, count in ((eh_ref, m2, 2), (ef_ref, m4, 4)):
            inv = lax.rsqrt(m + EPS)
            for c in range(count):
                ref[:, c * C : (c + 1) * C] = parts[c] * inv

    @pl.when(keeps)
    def _():
        near = ctx - z < SLOTS
        blk32[...] = jnp.zeros_like(blk32)

        @pl.when(near)
        def _():
            blk32[...] = zs[rows_of(((ctx - z) // NX) * 16 % 48, 16), :].astype(F32)

        @pl.loop(first_z, last_z + 1)
        def _(zz):
            @pl.when(zz != z)
            def _():
                pz_wait(zz).wait_recv()
                blk32[...] += rz[zz].astype(F32)
        embed(blk32[...])

    @pl.when(sends_b)
    def _():
        pb_copy(ctx).wait_recv()
        embed(rb[...].astype(F32))

    @pl.when(ctx == LAST)
    def _():
        embed(s2b[(HALF - 1) * 16 : HALF * 16, :].astype(F32))

    total = total_of(gx, NX * nc, x_pairs)
    qgain_ref[...] = total[0:1]
    kgain_ref[...] = total[1:2]

    @pl.loop(0, G)
    def _(g):
        for i in range(4):
            halo_copy(g, i).wait_send()
            grad_copy(g, i).wait_send()
    row_copy(0).wait_send()
    row_copy(1).wait_send()

    def sent(w):
        for i in (1, NX - 1):
            cx_copy(w, i).wait_send()

        @pl.when(z + w != ctx)
        def _():
            pz_copy(w).wait_send()

    each_slot(sent)
    by_column(NX - 1, lambda w: cf_copy(w, 0).wait_send())
    by_column(1, lambda w: cf_copy(w, 1).wait_send())
    other_slots(lambda w: px_copy(w).wait_send())

    @pl.when(keeps)
    def _():
        each_z(lambda zz: cz_copy(zz).wait_send())

    @pl.when(sends_b)
    def _():
        cb_copy(ctx).wait_send()

    @pl.when(ctx == LAST)
    def _():
        @pl.loop(HALF, LAST)
        def _(c):
            pb_copy(c).wait_send()
    for pair in z_pairs + y_pairs + x_pairs:
        pair[0].wait_send()


def emit(*refs):
    srcs, dsts, held, sem = refs[:8], refs[8:16], refs[16:24], refs[24]
    moves = []
    for i in range(8):
        parts = 4 if i == 3 else 1
        size = srcs[i].shape[0] // parts
        for p in range(parts):
            at = pl.ds(p * size, size)
            n = len(moves)
            first = pltpu.make_async_copy(srcs[i].at[at], held[i].at[at], sem.at[0, n])
            moves.append((first, pltpu.make_async_copy(held[i].at[at], dsts[i].at[at], sem.at[1, n])))
    order = sorted(range(len(moves)), key=lambda n: not 3 <= n < 7)
    for n in order:
        moves[n][0].start()
    for n in order:
        moves[n][0].wait()
        moves[n][1].start()
    for n in order:
        moves[n][1].wait()


def body(queries, keys, values, doc_lengths, cotangent, query_gain, key_gain):
    nc = 2 if lax.axis_size("dp") > 1 else 1
    ny = lax.axis_size("dp") // nc
    vmem, dma = pltpu.VMEM, pltpu.SemaphoreType.DMA
    scratch = [
        vmem((T, W), BF16),
        vmem((T, G * T), BF16),
        vmem((T, G * T), BF16),
        vmem((G, 4, T, T), BF16),
        vmem((G, 3 * T, T), BF16),
        vmem((G, 3 * T, T), F32),
        vmem((G, T, 1), F32),
        vmem((G, 3 * T, T), BF16),
        vmem((G, R * T, T), BF16),
        vmem((G, R * T, T), F32),
        vmem((G, R * T, 1), F32),
        vmem((G, R * T, 3 * T), F32),
        vmem((T, 3 * T), F32),
        vmem((T, W), F32),
        vmem((T, W), F32),
        vmem((T, W), BF16),
        vmem((2, 1, W), F32),
        vmem((2, 1, W), F32),
        vmem((16, C), F32),
        vmem((32, C), BF16),
        vmem((SLOTS * 32, C), BF16),
        vmem((HALF * 32, C), BF16),
        vmem((SLOTS * 16, C), BF16),
        vmem((HALF * 16, C), BF16),
        vmem((NX, 48, C), BF16),
        vmem((48, C), BF16),
        vmem((NZ, 16, C), BF16),
        vmem((16, C), BF16),
        vmem((R * T, 3 * T), BF16),
        vmem((G, R * T, 3 * T), BF16),
        vmem((R * T, T), BF16),
        vmem((G, R * T, T), F32),
        vmem((G, 4, T, T), BF16),
        vmem((G, 4, T, T), BF16),
        vmem((G, T, T), F32),
        vmem((G, T, T), F32),
        vmem((NZ, 8, T), F32),
        vmem((ny, 8, T), F32),
        vmem((nc * NX, 8, T), F32),
        dma((3,)),
        dma((G, 4)), dma((G, 4)),
        dma((2,)), dma((2,)),
        dma((NZ,)), dma((SLOTS,)),
        dma((SLOTS, NX)), dma((SLOTS,)),
        dma((SLOTS,)), dma((SLOTS, 2)),
        dma((1,)), dma((HALF,)),
        dma((SLOTS,)), dma((NX, 3)),
        dma((3,)), dma((NZ,)),
        dma((HALF,)), dma((1,)),
        dma((G, 4)), dma((G, 4)),
        dma((NZ,)), dma((NZ,)),
        dma((ny,)), dma((ny,)),
        dma((nc * NX,)), dma((nc * NX,)),
    ]
    shape = jax.ShapeDtypeStruct
    outs = pl.pallas_call(
        functools.partial(kernel, ny, nc),
        out_shape=(
            shape((4, C), F32),
            shape((4, 2 * C), F32),
            shape((4, W), F32),
            shape((T, W), BF16),
            shape((T, G * T), BF16),
            shape((T, G * T), BF16),
            shape((1, T), F32),
            shape((1, T), F32),
        ),
        in_specs=[pl.BlockSpec(memory_space=pl.ANY)] * 3 + [pl.BlockSpec(memory_space=pltpu.VMEM)] * 4,
        out_specs=tuple([pl.BlockSpec(memory_space=pltpu.VMEM)] * 8),
        scratch_shapes=scratch,
        compiler_params=pltpu.CompilerParams(
            collective_id=0, has_side_effects=True, vmem_limit_bytes=56 * 1024 * 1024
        ),
    )(
        queries[0], keys[0], values[0], doc_lengths, cotangent[0],
        query_gain.reshape(1, T), key_gain.reshape(1, T),
    )
    outs = pl.pallas_call(
        emit,
        out_shape=tuple(shape(out.shape, out.dtype) for out in outs),
        in_specs=[pl.BlockSpec(memory_space=pl.ANY)] * 8,
        out_specs=tuple([pl.BlockSpec(memory_space=pl.ANY)] * 8),
        scratch_shapes=[vmem(out.shape, out.dtype) for out in outs] + [dma((2, 11))],
    )(*outs)
    eq, eh, ef, gq, gk, gv, qgain, kgain = outs
    return (eq[None], eh[None], ef[None], gq[None], gk[None], gv[None], qgain[0], kgain[0])


def solution(mesh):
    rows = P("dp", "ctx", None)
    in_specs = (rows, rows, rows, P("dp", None), rows, P(), P())
    out_specs = (rows, rows, rows, rows, rows, rows, P(), P())
    return jax.shard_map(body, mesh=mesh, in_specs=in_specs, out_specs=out_specs, check_vma=False)
```
